512 devices in a mesh: elem: 64 (over x, y_lo, z), band: 8 (over y_hi, core).
Axes of the slice: x: 4, y: 8 (y_hi: 4, y_lo: 2; y = y_hi * 2 + y_lo), z: 8, core: 2. Of those that a mesh axis runs over, the one named last changes fastest.
Arguments:
- start_bands: bfloat16 [384, 256, 1024], P('elem', None, 'band'), may hold values from -6 to 6
- blocks: bfloat16 [384, 5, 256, 256], P('elem'), may hold values from -0.125 to 0.125
- neighbours: int32 [384, 5], P('elem'), may hold values from 0 to 383, as said below
- band_order: int32 [1024], replicated, may hold values from 0 to 1023, each once
- rotation: bfloat16 [1024, 1024], P('elem', 'band'), may hold values from -0.1875 to 0.1875
Outputs:
- final_bands: bfloat16 [384, 256, 1024], P('elem', None, 'band')
The draws below stay inside these ranges and needn't reach their ends.
Inputs may be any that keep to these rules, and one draw needn't show every extreme that they name: `neighbours`: the elements form a periodic grid of 128 columns of 3 elements; column c holds the ids c * 3 to c * 3 + 2 in a drawn order. Row e lists e, the element at the same place in the previous column, the one in the next column, then the previous and the next element within e's column, periodically, in that order. `band_order`: A permutation of the band numbers.
All inputs are finite; a program needn't handle non-finite values.
Results may differ from the reference program's by a relative error of at most 0.01.
Values may be sent and summed in bfloat16 or wider, within the bound.
A program may use at most 64 MiB of HBM per device.

```python
import jax
import jax.numpy as jnp
from jax import lax

NB = 256
M = 1024
GY = 3
NGX = 128
ELEMS = 384


def draw_neighbours(key, part):
    column_keys = jax.random.split(jax.random.fold_in(key, 71), NGX)
    placing = jax.vmap(lambda single_key: jax.random.permutation(single_key, GY))(column_keys).astype(jnp.int32)
    columns = jnp.arange(NGX, dtype=jnp.int32)[:, None] * GY
    id_grid = columns + placing
    previous_col = jnp.roll(id_grid, 1, axis=0)
    next_col = jnp.roll(id_grid, -1, axis=0)
    previous_row = jnp.roll(id_grid, 1, axis=1)
    next_row = jnp.roll(id_grid, -1, axis=1)
    links = jnp.stack([id_grid, previous_col, next_col, previous_row, next_row], axis=-1).reshape(NGX * GY, 5)
    result = jnp.zeros((NGX * GY, 5), jnp.int32)
    return result.at[id_grid.reshape(-1)].set(links)


def shard_levels(own_key, shape, cuts, smallest, largest):
    factor_of, own = 1.0, jax.random.fold_in(own_key, 6)
    for dim, parts in cuts:
        draws = jnp.exp(jax.random.uniform(jax.random.fold_in(own, dim), (parts,), jnp.float32, smallest / len(cuts), largest / len(cuts)))
        factor_of = factor_of * jnp.repeat(draws, shape[dim] // parts).reshape([-1 if axis == dim else 1 for axis in range(len(shape))])
    return factor_of


def scatter_about(stream_key, dims, spread, limit, cuts=(), held_as=jnp.bfloat16):
    values = jax.random.normal(stream_key, dims, jnp.float32) * spread
    if len(cuts) > 0:
        values = shard_levels(stream_key, dims, cuts, -0.22, 0.18) * values
    return jnp.clip(values, min=-limit, max=limit).astype(held_as)


def setup_inputs(seed: int = 0) -> dict:
    streams_of = jax.random.split(jax.random.key(seed), 6)
    start_bands = scatter_about(streams_of[0], (ELEMS, NB, M), 1.0, 6.0, ((0, 64), (2, 8)))
    blocks = scatter_about(streams_of[1], (ELEMS, 5, NB, NB), (10 * NB) ** -0.5, 0.125, ((0, 64),))
    neighbours = draw_neighbours(jax.random.fold_in(streams_of[5], 71), 0)
    band_order = jax.random.permutation(streams_of[3], M).astype(jnp.int32)
    rotation = scatter_about(streams_of[4], (M, M), M ** -0.5, 0.1875, ((0, 64), (1, 8)))
    return {"start_bands": start_bands, "blocks": blocks, "neighbours": neighbours, "band_order": band_order, "rotation": rotation}


def apply_blocks(current, blocks, neighbours):
    def single(args):
        element_blocks, element_links = args
        picked = current[element_links]
        left = element_blocks.transpose(1, 0, 2).reshape(NB, 5 * NB)
        return jnp.dot(left, picked.reshape(5 * NB, M), preferred_element_type=jnp.float32)
    return lax.map(single, (blocks, neighbours))


def chebyshev(initial, blocks, neighbours):
    first_term = apply_blocks(initial, blocks, neighbours).astype(jnp.bfloat16)
    second_term = (2.0 * apply_blocks(first_term, blocks, neighbours) - initial.astype(jnp.float32)).astype(jnp.bfloat16)
    third_term = (2.0 * apply_blocks(second_term, blocks, neighbours) - first_term.astype(jnp.float32)).astype(jnp.bfloat16)
    return third_term


def reference(start_bands, blocks, neighbours, band_order, rotation):
    filtered = chebyshev(start_bands, blocks, neighbours)
    permuted = filtered[:, :, band_order].reshape(ELEMS * NB, M)
    rotated = jnp.dot(permuted, rotation, preferred_element_type=jnp.float32).astype(jnp.bfloat16)
    rotated = rotated.reshape(ELEMS, NB, M)
    return chebyshev(rotated, blocks, neighbours)
```

```python
import functools

import jax
import jax.numpy as jnp
from jax import lax
from jax.experimental import pallas as pl
from jax.experimental.pallas import tpu as pltpu
from jax.sharding import PartitionSpec as P

MESH = pl.DeviceIdType.MESH
GY = 3
LANES = 128
SIZES = dict(X=4, YL=2, Z=8, YH=4)


def kernel(X, YL, Z, YH, start, blocks, links, order, rotation, out, blk, perm, rot, rotp, racc, *rest):
    bf16, f32 = jnp.bfloat16, jnp.float32
    rest = list(rest)

    def take(n):
        got, rest[:] = rest[:n], rest[n:]
        return got

    own = [take(2) for _ in range(6)]
    near = [take(2) for _ in range(6)]
    far = [take(2) for _ in range(6)]
    acc = take(2)
    filt = [take(2) for _ in range(2)]
    gath = take(2)
    back = take(2)
    (s_blk, s_init, r_own, s_halo, r_halo, s_rot, r_rot, l_rot, s_a2a, r_a2a, l_a2a, s_out, r_out, l_out) = rest

    E = X * YL * Z
    Y = YH * YL
    nb = blk.shape[2]
    part = nb // YH
    elem, band = lax.axis_index("elem"), lax.axis_index("band")
    core, yh = band % 2, band // 2
    z, yl, x = elem % Z, (elem // Z) % YL, elem // (Z * YL)
    y = yh * YL + yl
    partner = (elem, yh * 2 + 1 - core)
    zelem = (elem - 1 + 2 * core + E) % E
    zpeer = (zelem, yh * 2 + 1 - core)
    zother = ((elem + 1 - 2 * core + E) % E, band)
    mine, theirs = GY * core, GY * (1 - core)

    def remote(src, dst, ss, rs, dev):
        return pltpu.make_async_remote_copy(
            src_ref=src, dst_ref=dst, send_sem=ss, recv_sem=rs, device_id=dev, device_id_type=MESH
        )

    def wait(ref, sem):
        pltpu.make_async_copy(ref, ref, sem).wait()

    for i in range(GY):
        pltpu.make_async_copy(blocks.at[mine + i], blk.at[i], s_blk.at[i]).start()
    pltpu.make_async_copy(rotation, rot.at[core, x, y, z], l_rot).start()
    for k in range(2):

        @pl.when(core == k)
        def _():
            pltpu.make_async_copy(start.at[pl.ds(mine, GY)], own[0][k], r_own.at[k]).start()
            pltpu.make_async_copy(start.at[pl.ds(theirs, GY)], near[0][k], r_halo.at[0, k, 0]).start()

    z_peers = [(elem - z + (z + d) % Z, band) for d in range(1, Z)]
    y_peers = []
    for d in range(1, Y):
        other = (y + d) % Y
        y_peers.append(((x * YL + other % YL) * Z + z, (other // YL) * 2 + core))
    x_peers = [((((x + d) % X) * YL + yl) * Z + z, band) for d in range(1, X)]
    a_peers = [(elem, ((yh + d) % YH) * 2 + core) for d in range(1, YH)]

    barrier = pltpu.get_barrier_semaphore()
    greeted = [partner] + z_peers + y_peers + x_peers
    for step in (1, E - 1):
        for c in range(2):
            greeted.append(((elem + step) % E, yh * 2 + c))
    for dev in greeted:
        pl.semaphore_signal(barrier, inc=1, device_id=dev, device_id_type=MESH)
    pl.semaphore_wait(barrier, len(greeted))

    for k in range(2):
        sends = [
            remote(start.at[pl.ds(mine, GY)], far[0][k], s_init.at[0], r_halo.at[0, k, 1], zpeer),
            remote(start.at[pl.ds(theirs, GY)], far[0][k], s_init.at[1], r_halo.at[0, k, 1], zother),
            remote(start.at[pl.ds(theirs, GY)], own[0][k], s_init.at[2], r_own.at[k], partner),
            remote(start.at[pl.ds(mine, GY)], near[0][k], s_init.at[3], r_halo.at[0, k, 0], partner),
        ]

        @pl.when(core == k)
        def _():
            for copy in sends:
                copy.start()

    for dev in z_peers:
        remote(rotation, rot.at[core, x, y, z], s_rot.at[0], r_rot.at[0], dev).start()

    kts, width = perm.shape[0], perm.shape[3]

    def one_hot(step, carry):
        kt, xx = step // X, step % X
        k, yp = kt // (YH // 2), kt % (YH // 2)
        for h in range(2):
            rows = lax.broadcasted_iota(jnp.int32, (LANES, LANES), 0) + ((2 * yp + h) * 2 + k) * LANES
            for j in range(width // LANES):
                wanted = order[pl.ds(xx * (width // LANES) + j, 1), :]
                hit = jnp.where(rows == wanted, 1.0, 0.0).astype(bf16)
                perm[kt, xx, h * LANES : (h + 1) * LANES, j * LANES : (j + 1) * LANES] = hit
        return carry

    lax.fori_loop(0, kts * X, one_hot, 0)

    t_near, t_far = 2 - core, 1 + core

    def before(st, k):
        def one(i, carry):
            row = mine + i
            total = jnp.dot(blk[i, t_near], near[st][k][lax.rem(links[row, t_near], GY)], preferred_element_type=f32)
            for t in (0, 3, 4):
                total += jnp.dot(blk[i, t], own[st][k][lax.rem(links[row, t], GY)], preferred_element_type=f32)
            acc[k][i] = total
            return carry

        lax.fori_loop(0, GY, one, 0)

    def halo(st, k, i):
        src = own[st][k].at[i]
        return (
            remote(src, far[st][k].at[i], s_halo.at[st, k, 1], r_halo.at[st, k, 1], zpeer),
            remote(src, near[st][k].at[i], s_halo.at[st, k, 0], r_halo.at[st, k, 0], partner),
        )

    def after(st, k):
        f, last = st // 3, st % 3 == 2

        def one(i, carry):
            row = mine + i
            total = acc[k][i] + jnp.dot(
                blk[i, t_far], far[st][k][lax.rem(links[row, t_far], GY)], preferred_element_type=f32
            )
            if st % 3:
                total = 2.0 * total - own[st - 1][k][i].astype(f32)
            (filt[f] if last else own[st + 1])[k][i] = total.astype(bf16)
            if not last:
                for copy in halo(st + 1, k, i):
                    copy.start()
            return carry

        lax.fori_loop(0, GY, one, 0)

    def exchange(k, d):
        q = (yh + d) % YH
        return remote(
            filt[0][k].at[:, pl.ds(q * part, part), :], gath[k].at[yh], s_a2a.at[0, k], r_a2a.at[0, k], a_peers[d - 1]
        )

    def give_back(k, d):
        q = (yh + d) % YH
        return remote(
            back[k].at[q], own[3][k].at[:, pl.ds(yh * part, part), :], s_a2a.at[1, k], r_a2a.at[1, k], a_peers[d - 1]
        )

    for k in range(2):
        wait(own[0][k], r_own.at[k])
        wait(near[0][k], r_halo.at[0, k, 0])
        if k == 0:
            for i in range(GY):
                wait(blk.at[i], s_blk.at[i])
        before(0, k)
    for k in range(2):
        wait(far[0][k], r_halo.at[0, k, 1])
        after(0, k)
    wait(rot.at[core, x, y, z], l_rot)
    wait(rot.at[core, x, y, pl.ds(0, Z - 1)], r_rot.at[0])
    for dev in y_peers:
        remote(rot.at[core, x, y], rot.at[core, x, y], s_rot.at[1], r_rot.at[1], dev).start()
    for st in (1, 2):
        for k in range(2):
            wait(near[st][k], r_halo.at[st, k, 0])
            before(st, k)
        for k in range(2):
            wait(far[st][k], r_halo.at[st, k, 1])
            after(st, k)
            if st == 2:
                for d in range(1, YH):
                    exchange(k, d).start()
                mine_part = filt[0][k].at[:, pl.ds(yh * part, part), :]
                pltpu.make_async_copy(mine_part, gath[k].at[yh], l_a2a.at[0, k]).start()
        if st == 1:
            wait(rot.at[core, x, pl.ds(0, Y - 1)], r_rot.at[1])
            for dev in x_peers:
                remote(rot.at[core, x], rot.at[core, x], s_rot.at[2], r_rot.at[2], dev).start()

    wait(rot.at[core, pl.ds(0, X - 1)], r_rot.at[2])
    swap = remote(rot.at[core], rot.at[core], s_rot.at[3], r_rot.at[3], partner)
    swap.start()
    wait(rot.at[core], r_rot.at[3])
    half = YH // 2

    def permute(step, carry):
        kt, nt = step // kts, step % kts
        k, yp = nt // half, nt % half
        total = None
        for xx in range(X):
            sides = [rot[k, xx, pl.ds((2 * yp + h) * YL, YL)].reshape(width, LANES) for h in range(2)]
            term = jnp.dot(perm[kt, xx], jnp.concatenate(sides, axis=1), preferred_element_type=f32)
            total = term if total is None else total + term
        rotp[kt, nt] = total.astype(bf16)
        return carry

    lax.fori_loop(0, kts * kts, permute, 0)

    def product(k, nt):
        total = None
        for yp in range(half):
            sides = [gath[k][2 * yp + h].reshape(GY * part, LANES) for h in range(2)]
            term = jnp.dot(jnp.concatenate(sides, axis=1), rotp[k * half + yp, nt], preferred_element_type=f32)
            total = term if total is None else total + term
        return total

    for k in range(2):
        wait(gath[k].at[0], l_a2a.at[0, k])
        wait(gath[k].at[pl.ds(0, YH - 1)], r_a2a.at[0, k])
        if k == 0:

            def partial(nt, carry):
                racc[nt] = product(0, nt)
                return carry

            lax.fori_loop(0, kts, partial, 0)
    for k in range(2):

        def finish(yp, carry):
            total = (racc[k * half + yp] + product(1, k * half + yp)).astype(bf16)
            for h in range(2):
                back[k][2 * yp + h] = total[:, h * LANES : (h + 1) * LANES].reshape(GY, part, LANES)
            return carry

        lax.fori_loop(0, half, finish, 0)
        for d in range(1, YH):
            give_back(k, d).start()
        pltpu.make_async_copy(back[k].at[yh], own[3][k].at[:, pl.ds(yh * part, part), :], l_a2a.at[1, k]).start()

    for k in range(2):
        wait(gath[k].at[0], l_a2a.at[1, k])
        wait(gath[k].at[pl.ds(0, YH - 1)], r_a2a.at[1, k])
        for i in range(GY):
            for copy in halo(3, k, i):
                copy.start()
        wait(near[3][k], r_halo.at[3, k, 0])
        before(3, k)
    for st in (3, 4, 5):
        if st > 3:
            for k in range(2):
                wait(near[st][k], r_halo.at[st, k, 0])
                before(st, k)
        for k in range(2):
            wait(far[st][k], r_halo.at[st, k, 1])
            after(st, k)
            if st == 5:
                here = out.at[pl.ds(mine, GY)]

                @pl.when(core == k)
                def _():
                    pltpu.make_async_copy(filt[1][k], here, l_out).start()

                @pl.when(core != k)
                def _():
                    remote(filt[1][k], here, s_out, r_out, partner).start()

    wait(out.at[pl.ds(mine, GY)], l_out)
    wait(out.at[pl.ds(theirs, GY)], r_out)
    wait(filt[1][0], s_out)
    for j in range(4):
        wait(own[0][0], s_init.at[j])
    for st in range(1, 6):
        for k in range(2):
            for side in range(2):
                wait(own[st][k], s_halo.at[st, k, side])
    wait(rot.at[core, x, y, pl.ds(0, Z - 1)], s_rot.at[0])
    wait(rot.at[core, x, pl.ds(0, Y - 1)], s_rot.at[1])
    wait(rot.at[core, pl.ds(0, X - 1)], s_rot.at[2])
    wait(rot.at[core], s_rot.at[3])
    for j in range(2):
        for k in range(2):
            wait(gath[k].at[pl.ds(0, YH - 1)], s_a2a.at[j, k])


def build(mesh, X, YL, Z, YH):
    Y = YH * YL

    def body(start, blocks, neighbours, band_order, rotation):
        nb = start.shape[1]
        bands = band_order.shape[0]
        rows = rotation.shape[0]
        part = nb // YH
        kts = YH
        bf16 = jnp.bfloat16
        column = pltpu.VMEM((GY, nb, LANES), bf16)
        dma = pltpu.SemaphoreType.DMA
        hbm = pl.BlockSpec(memory_space=pl.ANY)
        return pl.pallas_call(
            functools.partial(kernel, X, YL, Z, YH),
            out_shape=jax.ShapeDtypeStruct(start.shape, bf16),
            in_specs=[
                hbm,
                hbm,
                pl.BlockSpec(memory_space=pltpu.SMEM),
                pl.BlockSpec(memory_space=pltpu.VMEM),
                hbm,
            ],
            out_specs=hbm,
            scratch_shapes=[
                pltpu.VMEM((GY, 5, nb, nb), bf16),
                pltpu.VMEM((kts, X, 2 * LANES, bands // X), bf16),
                pltpu.VMEM((2, X, Y, Z, rows, LANES), bf16),
                pltpu.VMEM((kts, kts, 2 * LANES, 2 * LANES), bf16),
                pltpu.VMEM((kts, GY * part, 2 * LANES), jnp.float32),
                *[column] * 36,
                *[pltpu.VMEM((GY, nb, LANES), jnp.float32)] * 2,
                *[column] * 4,
                *[pltpu.VMEM((YH, GY, part, LANES), bf16)] * 4,
                dma((GY,)),
                dma((4,)),
                dma((2,)),
                dma((6, 2, 2)),
                dma((6, 2, 2)),
                dma((4,)),
                dma((4,)),
                dma,
                dma((2, 2)),
                dma((2, 2)),
                dma((2, 2)),
                dma,
                dma,
                dma,
            ],
            compiler_params=pltpu.CompilerParams(collective_id=0, has_side_effects=True),
        )(start, blocks, neighbours, band_order.reshape(bands // LANES, LANES), rotation)

    return jax.shard_map(
        body,
        mesh=mesh,
        in_specs=(
            P("elem", None, "band"),
            P("elem", None, None, None),
            P("elem", None),
            P(),
            P("elem", "band"),
        ),
        out_specs=P("elem", None, "band"),
        check_vma=False,
    )


def solution(mesh):
    return build(mesh, **SIZES)
```

```python
import functools

import jax
import jax.numpy as jnp
from jax import lax
from jax.experimental import pallas as pl
from jax.experimental.pallas import tpu as pltpu
from jax.sharding import PartitionSpec as P

MESH = pl.DeviceIdType.MESH
GY = 3
LANES = 128
SIZES = dict(X=4, YL=2, Z=8, YH=4)


def kernel(X, YL, Z, YH, start, blocks, links_in, order_in, rotation, out, blk, perm, rot, racc, turned, links, table, order, *rest):
    bf16, f32 = jnp.bfloat16, jnp.float32
    rest = list(rest)

    def take(n):
        got, rest[:] = rest[:n], rest[n:]
        return got

    own = [take(2) for _ in range(6)]
    near = [take(2) for _ in range(6)]
    far = [take(2) for _ in range(6)]
    acc = take(2)
    filt = take(2)
    gath = take(2)
    back = take(2)
    (
        (s_blk, s_small, s_init, r_own, s_near, r_near, s_far, r_far),
        (s_z, r_z, l_rot, s_y, r_y, s_slab, r_slab, s_x, r_x, s_core, r_core),
        (s_a2a, r_a2a, l_a2a, s_out, r_out, l_out),
    ) = rest[:8], rest[8:19], rest[19:]

    E = X * YL * Z
    Y = YH * YL
    nb = blk.shape[2]
    part = nb // YH
    half = YH // 2
    elem, band = lax.axis_index("elem"), lax.axis_index("band")
    core, yh = lax.rem(band, 2), lax.div(band, 2)
    z, yl, x = lax.rem(elem, Z), lax.rem(lax.div(elem, Z), YL), lax.div(elem, Z * YL)
    y = yh * YL + yl
    twin = yh * 2 + 1 - core
    partner = (elem, twin)
    zpeer = (lax.rem(elem - 1 + 2 * core + E, E), twin)
    zother = (lax.rem(elem + 1 - 2 * core + E, E), band)
    mine, theirs = GY * core, GY * (1 - core)

    def remote(src, dst, ss, rs, dev):
        return pltpu.make_async_remote_copy(
            src_ref=src, dst_ref=dst, send_sem=ss, recv_sem=rs, device_id=dev, device_id_type=MESH
        )

    def wait(ref, sem):
        pltpu.make_async_copy(ref, ref, sem).wait()

    z_peers = [(elem - z + lax.rem(z + d, Z), band) for d in range(1, Z)]
    y_peers = []
    for d in range(1, Y):
        other = lax.rem(y + d, Y)
        y_peers.append(((x * YL + lax.rem(other, YL)) * Z + z, lax.div(other, YL) * 2 + core))
    x_peers = [((lax.rem(x + d, X) * YL + yl) * Z + z, band) for d in range(1, X)]
    a_peers = [(elem, lax.rem(yh + d, YH) * 2 + core) for d in range(1, YH)]

    barrier = pltpu.get_barrier_semaphore()
    greeted = [partner] + z_peers + y_peers + x_peers
    greeted += [(elem, lax.rem(yh + d, YH) * 2 + 1 - core) for d in range(1, YH)]
    for step in (1, E - 1):
        for c in range(2):
            greeted.append((lax.rem(elem + step, E), yh * 2 + c))
    for dev in greeted:
        pl.semaphore_signal(barrier, inc=1, device_id=dev, device_id_type=MESH)

    pltpu.make_async_copy(links_in, links, s_small.at[0]).start()
    pltpu.make_async_copy(order_in, order, s_small.at[1]).start()
    for k in range(2):

        @pl.when(core == k)
        def _():
            pltpu.make_async_copy(start.at[pl.ds(mine, GY)], own[0][k], r_own.at[k]).start()
            pltpu.make_async_copy(start.at[pl.ds(theirs, GY)], near[0][k], r_near.at[0, k]).start()

    for i in range(GY):
        pltpu.make_async_copy(blocks.at[mine + i], blk.at[i], s_blk.at[i]).start()
    pl.semaphore_wait(barrier, len(greeted))

    def at_end(c):
        return jnp.logical_or(c == 0, c == Z - 1)

    end_plane = at_end(z)
    inner_plane = jnp.logical_not(end_plane)

    @pl.when(inner_plane)
    def _():
        pltpu.make_async_copy(rotation, rot.at[core, x, y, z], l_rot).start()

    for d, dev in enumerate(z_peers):

        @pl.when(jnp.logical_not(at_end(lax.rem(z + d + 1, Z))))
        def _():
            remote(rotation, rot.at[core, x, y, z], s_z, r_z, dev).start()

    def first_far(k):
        remote(start.at[pl.ds(mine, GY)], far[0][k], s_init.at[0], r_far.at[0, k, 0], zpeer).start()
        remote(start.at[pl.ds(theirs, GY)], far[0][k], s_init.at[1], r_far.at[0, k, 0], zother).start()

    for k in range(2):

        @pl.when(core == k)
        def _():
            first_far(k)
            remote(start.at[pl.ds(theirs, GY)], own[0][k], s_init.at[2], r_own.at[k], partner).start()
            remote(start.at[pl.ds(mine, GY)], near[0][k], s_init.at[3], r_near.at[0, k], partner).start()

    wait(links, s_small.at[0])
    wait(order, s_small.at[1])
    t_near, t_far = 2 - core, 1 + core

    def place(row, t):
        return lax.rem(links[row, t], GY)

    def slot_of(c, e):
        return jnp.where(c == 1, place(GY + e, 2), e)

    for j in range(GY):
        e = jnp.where(
            core == 0,
            j,
            jnp.where(place(GY, 2) == j, 0, jnp.where(place(GY + 1, 2) == j, 1, 2)),
        )
        for v, at in ((0, e), (1, e), (2, j)):
            row = mine + at
            ids = (place(row, 3), place(row, 4), place(row, t_near), place(row, t_far))
            if v == 0:
                line = (at, at, *ids)
            else:
                here = j if v == 1 else slot_of(core, at)
                line = (at, here, slot_of(core, ids[0]), slot_of(core, ids[1]), slot_of(1 - core, ids[2]), here)
            for n, value in enumerate(line):
                table[v, j * 6 + n] = value

    kts, width = perm.shape[0], perm.shape[3]

    def one_hot(step, carry):
        kt, xx = lax.div(step, X), lax.rem(step, X)
        k, yp = lax.div(kt, half), lax.rem(kt, half)
        for h in range(2):
            rows = lax.broadcasted_iota(jnp.int32, (LANES, LANES), 0) + ((2 * yp + h) * 2 + k) * LANES
            for j in range(width // LANES):
                wanted = order[pl.ds(xx * (width // LANES) + j, 1), :]
                hit = jnp.where(rows == wanted, 1.0, 0.0).astype(bf16)
                perm[kt, xx, h * LANES : (h + 1) * LANES, j * LANES : (j + 1) * LANES] = hit
        return carry

    def row_of(st):
        return 0 if st == 0 else 2 if st == 5 else 1

    def before(st, k):
        v = row_of(st)

        def one(j, carry):
            e = table[v, j * 6]
            total = jnp.dot(blk[e, t_near], near[st][k][table[v, j * 6 + 4]], preferred_element_type=f32)
            for n, t in ((1, 0), (2, 3), (3, 4)):
                total += jnp.dot(blk[e, t], own[st][k][table[v, j * 6 + n]], preferred_element_type=f32)
            acc[k][j] = total
            return carry

        lax.fori_loop(0, GY, one, 0)

    def halo(st, k, j):
        src = own[st][k].at[j]
        remote(src, far[st][k].at[j], s_far.at[st, k], r_far.at[st, k, j], zpeer).start()
        remote(src, near[st][k].at[j], s_near.at[st, k], r_near.at[st, k], partner).start()

    def exchange(k, j):
        for d in range(1, YH):
            q = lax.rem(yh + d, YH)
            src = filt[k].at[j, pl.ds(q * part, part)]
            remote(src, gath[k].at[yh, j], s_a2a.at[k], r_a2a.at[k], a_peers[d - 1]).start()
        src = filt[k].at[j, pl.ds(yh * part, part)]
        pltpu.make_async_copy(src, gath[k].at[yh, j], l_a2a.at[k]).start()

    def after(st, k):
        v = row_of(st)
        if st == 0:
            wait(far[0][k], r_far.at[0, k, 0])
        if st == 5:
            for j in range(GY):
                wait(far[st][k].at[j], r_far.at[st, k, j])

        def one(j, carry):
            e = table[v, j * 6]
            if st in (0, 5):
                there = far[st][k][table[v, j * 6 + 5]]
            else:
                wait(far[st][k].at[j], r_far.at[st, k, j])
                there = far[st][k][j]
            total = acc[k][j] + jnp.dot(blk[e, t_far], there, preferred_element_type=f32)
            if st % 3:
                previous = own[st - 1][k][e if st == 1 else table[v, j * 6 + 1]]
                total = 2.0 * total - previous.astype(f32)
            if st < 5:
                own[st + 1][k][j] = total.astype(bf16)
                halo(st + 1, k, j)
            else:
                filt[k][j] = total.astype(bf16)
                exchange(k, j)
            return carry

        lax.fori_loop(0, GY, one, 0)

    def early(st, k):
        wait(near[st][k], r_near.at[st, k])
        before(st, k)

    lax.fori_loop(0, kts * X, one_hot, 0)
    wait(own[0][0], r_own.at[0])
    wait(near[0][0], r_near.at[0, 0])

    for i in range(GY):
        wait(blk.at[i], s_blk.at[i])
    before(0, 0)
    wait(own[0][1], r_own.at[1])
    early(0, 1)

    slab = rot.at[core, x]

    def along_y():
        wait(rot.at[core, x, y, z], l_rot)
        wait(rot.at[core, x, y, pl.ds(0, Z - 1)], r_z)
        at = rot.at[core, x, y]
        for d in range(1, Y):
            remote(at, at, s_y, r_y, y_peers[d - 1]).start()

    def along_x():
        for d in range(1, X):
            remote(slab, slab, s_x, r_x.at[d - 1], x_peers[d - 1]).start()
        remote(slab, slab, s_core, r_core.at[0], partner).start()

    pieces = [(yy, d) for yy in range(Y) for d in range(1, X)]

    def along_x_in_turn(turn, turns):
        @pl.when(end_plane)
        def _():
            if turn == 0:
                wait(slab, r_slab)
                remote(slab, slab, s_core, r_core.at[0], partner).start()
            for yy, d in pieces[turn * len(pieces) // turns : (turn + 1) * len(pieces) // turns]:
                at = rot.at[core, x, yy]
                remote(at, at, s_x, r_x.at[d - 1], x_peers[d - 1]).start()

    def hand_over():
        for d in range(1, X):
            at = rot.at[core, lax.rem(x - d + X, X)]
            wait(at, r_x.at[d - 1])
            remote(at, at, s_core, r_core.at[d], partner).start()

    for st in range(6):
        after(st, 0)
        if st == 0:
            pl.when(inner_plane)(along_y)
        if st == 1:

            @pl.when(inner_plane)
            def _():
                wait(rot.at[core, x, pl.ds(0, Y - 1)], r_y)

                @pl.when(z == 1)
                def _():
                    remote(slab, slab, s_slab.at[0], r_slab, (elem - 1, band)).start()

                @pl.when(z == Z - 2)
                def _():
                    remote(slab, slab, s_slab.at[1], r_slab, (elem + 1, band)).start()

                along_x()

        turn = 4 * (st - 2)
        if 2 <= st < 5:
            along_x_in_turn(turn, 12)
        if st == 4:
            pl.when(inner_plane)(hand_over)
        if st:
            early(st, 1)
        if 2 <= st < 5:
            along_x_in_turn(turn + 1, 12)
        after(st, 1)
        if 2 <= st < 5:
            along_x_in_turn(turn + 2, 12)
        if st < 5:
            early(st + 1, 0)
        if 2 <= st < 5:
            along_x_in_turn(turn + 3, 12)
    pl.when(end_plane)(hand_over)

    def reordered(k, xx):
        total = None
        for yp in range(half):
            sides = [gath[k][2 * yp + h].reshape(GY * part, LANES) for h in range(2)]
            term = jnp.dot(jnp.concatenate(sides, axis=1), perm[k * half + yp, xx], preferred_element_type=f32)
            total = term if total is None else total + term
        return total

    def first_half(xx, carry):
        racc[xx] = reordered(0, xx)
        return carry

    def second_half(xx, carry):
        turned[xx] = (racc[xx] + reordered(1, xx)).astype(bf16)
        return carry

    for k in range(2):
        wait(gath[k].at[0], l_a2a.at[k])
        wait(gath[k].at[pl.ds(0, YH - 1)], r_a2a.at[k])
        if k == 0:
            lax.fori_loop(0, X, first_half, 0)
    lax.fori_loop(0, X, second_half, 0)
    for d in range(X):
        wait(rot.at[core, 0], r_core.at[d])
    for k in range(2):
        for t in range(half):
            yp = lax.rem(lax.div(yh, 2) + 1 + t, half)
            total = None
            for xx in range(X):
                sides = [rot[k, xx, pl.ds((2 * yp + h) * YL, YL)].reshape(width, LANES) for h in range(2)]
                term = jnp.dot(turned[xx], jnp.concatenate(sides, axis=1), preferred_element_type=f32)
                total = term if total is None else total + term
            total = total.astype(bf16)
            for h in range(2):
                back[k][2 * yp + h] = total[:, h * LANES : (h + 1) * LANES].reshape(GY, part, LANES)
            landing = out.at[pl.ds(mine, GY), pl.ds(yh * part, part), :]
            if t < half - 1:
                goals = [2 * yp, 2 * yp + 1]
            else:
                goals = [yh + 1 - 2 * lax.rem(yh, 2)]

                @pl.when(core == k)
                def _():
                    pltpu.make_async_copy(back[k].at[yh], landing, l_out).start()

                @pl.when(core != k)
                def _():
                    remote(back[k].at[yh], landing, s_out, r_out, partner).start()

            for q in goals:
                remote(back[k].at[q], landing, s_out, r_out, (elem, q * 2 + k)).start()

    most = out.at[:, pl.ds(0, nb - part // 2), :]
    wait(back[0].at[0], l_out)
    wait(most, r_out)
    wait(most, s_out)
    for j in range(4):
        wait(own[0][0], s_init.at[j])
    for st in range(1, 6):
        for k in range(2):
            wait(own[st][k], s_far.at[st, k])
            wait(own[st][k], s_near.at[st, k])

    @pl.when(end_plane)
    def _():
        wait(rot.at[core, x, y, pl.ds(0, Z - 2)], s_z)

    @pl.when(inner_plane)
    def _():
        wait(rot.at[core, x, y, pl.ds(0, Z - 3)], s_z)
        wait(rot.at[core, x, pl.ds(0, Y - 1)], s_y)

    for n, plane in enumerate((1, Z - 2)):

        @pl.when(z == plane)
        def _():
            wait(slab, s_slab.at[n])

    wait(rot.at[core, pl.ds(0, X - 1)], s_x)
    wait(rot.at[core], s_core)
    for k in range(2):
        wait(gath[k].at[pl.ds(0, YH - 1)], s_a2a.at[k])


def build(mesh, X, YL, Z, YH):
    Y = YH * YL

    def body(start, blocks, neighbours, band_order, rotation):
        nb = start.shape[1]
        bands = band_order.shape[0]
        rows = rotation.shape[0]
        part = nb // YH
        kts = YH
        bf16 = jnp.bfloat16
        column = pltpu.VMEM((GY, nb, LANES), bf16)
        dma = pltpu.SemaphoreType.DMA
        hbm = pl.BlockSpec(memory_space=pl.ANY)
        return pl.pallas_call(
            functools.partial(kernel, X, YL, Z, YH),
            out_shape=jax.ShapeDtypeStruct(start.shape, bf16),
            in_specs=[hbm] * 5,
            out_specs=hbm,
            scratch_shapes=[
                pltpu.VMEM((GY, 5, nb, nb), bf16),
                pltpu.VMEM((kts, X, 2 * LANES, bands // X), bf16),
                pltpu.VMEM((2, X, Y, Z, rows, LANES), bf16),
                pltpu.VMEM((X, GY * part, bands // X), jnp.float32),
                pltpu.VMEM((X, GY * part, bands // X), bf16),
                pltpu.SMEM(neighbours.shape, jnp.int32),
                pltpu.SMEM((3, 6 * GY), jnp.int32),
                pltpu.VMEM((bands // LANES, LANES), jnp.int32),
                *[column] * 36,
                *[pltpu.VMEM((GY, nb, LANES), jnp.float32)] * 2,
                *[column] * 2,
                *[pltpu.VMEM((YH, GY, part, LANES), bf16)] * 4,
                *[dma((GY,)), dma((2,)), dma((4,)), dma((2,))],
                *[dma((6, 2)), dma((6, 2)), dma((6, 2)), dma((6, 2, GY))],
                *[dma, dma, dma, dma, dma, dma((2,)), dma, dma, dma((X - 1,)), dma, dma((X,))],
                *[dma((2,)), dma((2,)), dma((2,)), dma, dma, dma],
            ],
            compiler_params=pltpu.CompilerParams(collective_id=0, has_side_effects=True),
        )(start, blocks, neighbours, band_order.reshape(bands // LANES, LANES), rotation)

    return jax.shard_map(
        body,
        mesh=mesh,
        in_specs=(
            P("elem", None, "band"),
            P("elem", None, None, None),
            P("elem", None),
            P(),
            P("elem", "band"),
        ),
        out_specs=P("elem", None, "band"),
        check_vma=False,
    )


def solution(mesh):
    return build(mesh, **SIZES)
```

```python
import functools

import jax
import jax.numpy as jnp
from jax import lax
from jax.experimental import pallas as pl
from jax.experimental.pallas import tpu as pltpu
from jax.sharding import PartitionSpec as P

MESH = pl.DeviceIdType.MESH
GY = 3
LANES = 128
SIZES = dict(X=4, YL=2, Z=8, YH=4)


def kernel(X, YL, Z, YH, start, blocks, links_in, order_in, rotation, out, blk, perm, rot, racc, turned, first, links, table, order, *rest):
    bf16, f32 = jnp.bfloat16, jnp.float32
    rest = list(rest)

    def take(n):
        got, rest[:] = rest[:n], rest[n:]
        return got

    own = [take(2) for _ in range(6)]
    near = [take(2) for _ in range(6)]
    far = [take(2) for _ in range(6)]
    acc = take(2)
    filt = take(2)
    gath = take(2)
    back = take(2)
    (
        (s_blk, s_small, s_init, r_own, s_near, r_near, s_far, r_far),
        (s_z, r_z, l_rot, s_y, r_y, s_slab, r_slab, s_x, r_x, s_core, r_core),
        (s_a2a, r_a2a, l_a2a, s_out, r_out, l_out),
    ) = rest[:8], rest[8:19], rest[19:]

    E = X * YL * Z
    Y = YH * YL
    nb = blk.shape[2]
    part = nb // YH
    half = YH // 2
    elem, band = lax.axis_index("elem"), lax.axis_index("band")
    core, yh = lax.rem(band, 2), lax.div(band, 2)
    z, yl, x = lax.rem(elem, Z), lax.rem(lax.div(elem, Z), YL), lax.div(elem, Z * YL)
    y = yh * YL + yl
    twin = yh * 2 + 1 - core
    partner = (elem, twin)
    zpeer = (lax.rem(elem - 1 + 2 * core + E, E), twin)
    zother = (lax.rem(elem + 1 - 2 * core + E, E), band)
    mine, theirs = GY * core, GY * (1 - core)

    def remote(src, dst, ss, rs, dev):
        return pltpu.make_async_remote_copy(
            src_ref=src, dst_ref=dst, send_sem=ss, recv_sem=rs, device_id=dev, device_id_type=MESH
        )

    def wait(ref, sem):
        pltpu.make_async_copy(ref, ref, sem).wait()

    z_peers = [(elem - z + lax.rem(z + d, Z), band) for d in range(1, Z)]
    y_peers = []
    for d in range(1, Y):
        other = lax.rem(y + d, Y)
        y_peers.append(((x * YL + lax.rem(other, YL)) * Z + z, lax.div(other, YL) * 2 + core))
    x_peers = [((lax.rem(x + d, X) * YL + yl) * Z + z, band) for d in range(1, X)]
    a_peers = [(elem, lax.rem(yh + d, YH) * 2 + core) for d in range(1, YH)]

    barrier = pltpu.get_barrier_semaphore()
    greeted = [partner] + z_peers + y_peers + x_peers
    greeted += [(elem, lax.rem(yh + d, YH) * 2 + 1 - core) for d in range(1, YH)]
    for step in (1, E - 1):
        for c in range(2):
            greeted.append((lax.rem(elem + step, E), yh * 2 + c))
    for dev in greeted:
        pl.semaphore_signal(barrier, inc=1, device_id=dev, device_id_type=MESH)

    pltpu.make_async_copy(links_in, links, s_small.at[0]).start()
    pltpu.make_async_copy(order_in, order, s_small.at[1]).start()
    for k in range(2):

        @pl.when(core == k)
        def _():
            pltpu.make_async_copy(start.at[pl.ds(mine, GY)], own[0][k], r_own.at[k]).start()
            pltpu.make_async_copy(start.at[pl.ds(theirs, GY)], near[0][k], r_near.at[0, k]).start()

    for i in range(GY):
        pltpu.make_async_copy(blocks.at[mine + i], blk.at[i], s_blk.at[i]).start()
    wait(links, s_small.at[0])
    t_near, t_far = 2 - core, 1 + core

    def place(row, t):
        return lax.rem(links[row, t], GY)

    def slot_of(c, e):
        return jnp.where(c == 1, place(GY + e, 2), e)

    for j in range(GY):
        second = jnp.where(place(GY, 2) == j, 0, jnp.where(place(GY + 1, 2) == j, 1, 2))
        e = jnp.where(core == 0, j, second)
        row = mine + e
        ids = (place(row, 3), place(row, 4), place(row, t_near))
        slots = (slot_of(core, ids[0]), slot_of(core, ids[1]), slot_of(1 - core, ids[2]))
        for v, line in ((0, (e, e, *ids)), (1, (e, j, *slots))):
            for n, value in enumerate(line):
                table[v, j * 5 + n] = value
        table[2, j] = slot_of(core, j)
        table[2, GY + j] = second

    for k, column in ((0, near[0][0]), (1, own[0][1])):

        @pl.when(core == k)
        def _():
            wait(own[0][k], r_own.at[k])
            wait(near[0][k], r_near.at[0, k])
            for j in range(GY):
                first[j] = column[table[2, GY + j]]

    pl.semaphore_wait(barrier, len(greeted))

    def at_end(c):
        return jnp.logical_or(c == 0, c == Z - 1)

    end_plane = at_end(z)
    inner_plane = jnp.logical_not(end_plane)

    @pl.when(inner_plane)
    def _():
        pltpu.make_async_copy(rotation, rot.at[core, x, y, z], l_rot).start()

    for d, dev in enumerate(z_peers):

        @pl.when(jnp.logical_not(at_end(lax.rem(z + d + 1, Z))))
        def _():
            remote(rotation, rot.at[core, x, y, z], s_z, r_z, dev).start()

    def first_far(k):
        for j in range(GY):
            here = start.at[j]
            for n, (src, dev) in enumerate(((first.at[j] if k else here, zpeer), (here if k else first.at[j], zother))):
                remote(src, far[0][k].at[j], s_init.at[n], r_far.at[0, k, j], dev).start()

    for k in range(2):

        @pl.when(core == k)
        def _():
            if k == 0:
                first_far(k)
            remote(start.at[pl.ds(theirs, GY)], own[0][k], s_init.at[2], r_own.at[k], partner).start()
            remote(start.at[pl.ds(mine, GY)], near[0][k], s_init.at[3], r_near.at[0, k], partner).start()

    wait(order, s_small.at[1])

    kts, width = perm.shape[0], perm.shape[3]

    def one_hot(step, carry):
        kt, xx = lax.div(step, X), lax.rem(step, X)
        k, yp = lax.div(kt, half), lax.rem(kt, half)
        for h in range(2):
            rows = lax.broadcasted_iota(jnp.int32, (LANES, LANES), 0) + ((2 * yp + h) * 2 + k) * LANES
            for j in range(width // LANES):
                wanted = order[pl.ds(xx * (width // LANES) + j, 1), :]
                hit = jnp.where(rows == wanted, 1.0, 0.0).astype(bf16)
                perm[kt, xx, h * LANES : (h + 1) * LANES, j * LANES : (j + 1) * LANES] = hit
        return carry

    def row_of(st):
        return 0 if st == 0 else 1

    def before(st, k):
        v = row_of(st)

        def one(j, carry):
            e = table[v, j * 5]
            total = jnp.dot(blk[e, t_near], near[st][k][table[v, j * 5 + 4]], preferred_element_type=f32)
            for n, t in ((1, 0), (2, 3), (3, 4)):
                total += jnp.dot(blk[e, t], own[st][k][table[v, j * 5 + n]], preferred_element_type=f32)
            acc[k][j] = total
            return carry

        lax.fori_loop(0, GY, one, 0)

    def halo(st, k, j):
        src = own[st][k].at[j]
        remote(src, far[st][k].at[j], s_far.at[st, k], r_far.at[st, k, j], zpeer).start()
        remote(src, near[st][k].at[j], s_near.at[st, k], r_near.at[st, k], partner).start()

    def exchange(k, j):
        for d in range(1, YH):
            q = lax.rem(yh + d, YH)
            src = filt[k].at[j, pl.ds(q * part, part)]
            remote(src, gath[k].at[yh, j], s_a2a.at[k], r_a2a.at[k], a_peers[d - 1]).start()
        src = filt[k].at[j, pl.ds(yh * part, part)]
        pltpu.make_async_copy(src, gath[k].at[yh, j], l_a2a.at[k]).start()

    def after(st, k):
        v = row_of(st)
        def one(j, carry):
            e = table[v, j * 5]
            wait(far[st][k].at[j], r_far.at[st, k, j])
            total = acc[k][j] + jnp.dot(blk[e, t_far], far[st][k][j], preferred_element_type=f32)
            if st % 3:
                previous = own[st - 1][k][e if st == 1 else j]
                total = 2.0 * total - previous.astype(f32)
            if st < 5:
                own[st + 1][k][j] = total.astype(bf16)
                halo(st + 1, k, j)
            else:
                filt[k][j] = total.astype(bf16)
                exchange(k, j)
            return carry

        lax.fori_loop(0, GY, one, 0)

    def early(st, k):
        wait(near[st][k], r_near.at[st, k])
        before(st, k)

    lax.fori_loop(0, kts * X, one_hot, 0)

    @pl.when(core == 1)
    def _():
        wait(own[0][0], r_own.at[0])
        wait(near[0][0], r_near.at[0, 0])
        first_far(1)

    for i in range(GY):
        wait(blk.at[i], s_blk.at[i])
    before(0, 0)

    @pl.when(core == 0)
    def _():
        wait(own[0][1], r_own.at[1])
        wait(near[0][1], r_near.at[0, 1])

    before(0, 1)

    slab = rot.at[core, x]

    def along_y():
        wait(rot.at[core, x, y, z], l_rot)
        wait(rot.at[core, x, y, pl.ds(0, Z - 1)], r_z)
        at = rot.at[core, x, y]
        for d in range(1, Y):
            remote(at, at, s_y, r_y, y_peers[d - 1]).start()

    beside = [d for d in range(1, X) if d in (1, X - 1)]
    others = [d for d in range(1, X) if d not in beside]

    def to_end_plane(at, n, sem):
        for m, (plane, step) in enumerate(((1, -1), (Z - 2, 1))):

            @pl.when(z == plane)
            def _():
                remote(at, at, s_slab.at[n, m], sem, (elem + step, band)).start()

    def inner_spread():
        wait(rot.at[core, x, pl.ds(0, Y - 1)], r_y)
        to_end_plane(slab, 0, r_slab)
        for d in others + beside:
            remote(slab, slab, s_x.at[d - 1], r_x.at[d - 1], x_peers[d - 1]).start()
        remote(slab, slab, s_core, r_core.at[0], partner).start()

    pieces = [(yy, d) for yy in range(Y) for d in beside]

    def along_x_in_turn(turn):
        turns = 6

        @pl.when(end_plane)
        def _():
            if turn == 0:
                wait(slab, r_slab)
                remote(slab, slab, s_core, r_core.at[0], partner).start()
            for yy, d in pieces[turn * len(pieces) // turns : (turn + 1) * len(pieces) // turns]:
                at = rot.at[core, x, yy]
                remote(at, at, s_x.at[d - 1], r_x.at[d - 1], x_peers[d - 1]).start()

    def hand_over(ds):
        for d in ds:
            at = rot.at[core, lax.rem(x - d + X, X)]
            wait(at, r_x.at[d - 1])
            remote(at, at, s_core, r_core.at[d], partner).start()
            if d in others:
                to_end_plane(at, d, r_x.at[d - 1])

    for st in range(6):
        if st == 5:
            pl.when(inner_plane)(lambda: hand_over(others))
        after(st, 0)
        if st == 1:
            pl.when(inner_plane)(along_y)
        if st == 3:
            pl.when(inner_plane)(inner_spread)
        if st > 3:
            along_x_in_turn(4 * (st - 4))
        if st:
            early(st, 1)
        if st > 3:
            along_x_in_turn(4 * (st - 4) + 1)
        after(st, 1)
        if st == 4:
            along_x_in_turn(2)
        if st < 5:
            early(st + 1, 0)
        if st == 4:
            along_x_in_turn(3)
    hand_over(beside)
    pl.when(end_plane)(lambda: hand_over(others))

    def rows_of(k, q):
        return jnp.concatenate([gath[k][q, table[2, i]] for i in range(GY)], axis=0)

    def reordered(k, xx):
        total = None
        for yp in range(half):
            sides = [rows_of(k, 2 * yp + h) for h in range(2)]
            term = jnp.dot(jnp.concatenate(sides, axis=1), perm[k * half + yp, xx], preferred_element_type=f32)
            total = term if total is None else total + term
        return total

    def first_half(xx, carry):
        racc[xx] = reordered(0, xx)
        return carry

    def second_half(xx, carry):
        turned[xx] = (racc[xx] + reordered(1, xx)).astype(bf16)
        return carry

    for k in range(2):
        wait(gath[k].at[0], l_a2a.at[k])
        wait(gath[k].at[pl.ds(0, YH - 1)], r_a2a.at[k])
        if k == 0:
            lax.fori_loop(0, X, first_half, 0)
    lax.fori_loop(0, X, second_half, 0)
    for d in range(X):
        wait(rot.at[core, 0], r_core.at[d])
    for k in range(2):
        for t in range(half):
            yp = lax.rem(lax.div(yh, 2) + 1 + t, half)
            total = None
            for xx in range(X):
                sides = [rot[k, xx, pl.ds((2 * yp + h) * YL, YL)].reshape(width, LANES) for h in range(2)]
                term = jnp.dot(turned[xx], jnp.concatenate(sides, axis=1), preferred_element_type=f32)
                total = term if total is None else total + term
            total = total.astype(bf16)
            for h in range(2):
                back[k][2 * yp + h] = total[:, h * LANES : (h + 1) * LANES].reshape(GY, part, LANES)
            landing = out.at[pl.ds(mine, GY), pl.ds(yh * part, part), :]
            if t < half - 1:
                goals = [2 * yp, 2 * yp + 1]
            else:
                goals = [yh + 1 - 2 * lax.rem(yh, 2)]

                @pl.when(core == k)
                def _():
                    pltpu.make_async_copy(back[k].at[yh], landing, l_out).start()

                @pl.when(core != k)
                def _():
                    remote(back[k].at[yh], landing, s_out, r_out, partner).start()

            for q in goals:
                remote(back[k].at[q], landing, s_out, r_out, (elem, q * 2 + k)).start()

    most = out.at[:, pl.ds(0, nb - part // 2), :]
    wait(back[0].at[0], l_out)
    wait(most, r_out)
    wait(most, s_out)
    for j in range(4):
        wait(own[0][0], s_init.at[j])
    for st in range(1, 6):
        for k in range(2):
            wait(own[st][k], s_far.at[st, k])
            wait(own[st][k], s_near.at[st, k])

    @pl.when(end_plane)
    def _():
        wait(rot.at[core, x, y, pl.ds(0, Z - 2)], s_z)

    @pl.when(inner_plane)
    def _():
        wait(rot.at[core, x, y, pl.ds(0, Z - 3)], s_z)
        wait(rot.at[core, x, pl.ds(0, Y - 1)], s_y)

    for m, plane in enumerate((1, Z - 2)):

        @pl.when(z == plane)
        def _():
            for n in (0, *others):
                wait(slab, s_slab.at[n, m])

    for d in beside:
        wait(slab, s_x.at[d - 1])

    @pl.when(inner_plane)
    def _():
        for d in others:
            wait(slab, s_x.at[d - 1])

    wait(rot.at[core], s_core)
    for k in range(2):
        wait(gath[k].at[pl.ds(0, YH - 1)], s_a2a.at[k])


def build(mesh, X, YL, Z, YH):
    Y = YH * YL

    def body(start, blocks, neighbours, band_order, rotation):
        nb = start.shape[1]
        bands = band_order.shape[0]
        rows = rotation.shape[0]
        part = nb // YH
        kts = YH
        bf16 = jnp.bfloat16
        column = pltpu.VMEM((GY, nb, LANES), bf16)
        dma = pltpu.SemaphoreType.DMA
        hbm = pl.BlockSpec(memory_space=pl.ANY)
        return pl.pallas_call(
            functools.partial(kernel, X, YL, Z, YH),
            out_shape=pltpu.VMEM(start.shape, bf16),
            in_specs=[hbm] * 5,
            out_specs=hbm,
            scratch_shapes=[
                pltpu.VMEM((GY, 5, nb, nb), bf16),
                pltpu.VMEM((kts, X, 2 * LANES, bands // X), bf16),
                pltpu.VMEM((2, X, Y, Z, rows, LANES), bf16),
                pltpu.VMEM((X, GY * part, bands // X), jnp.float32),
                pltpu.VMEM((X, GY * part, bands // X), bf16),
                column,
                pltpu.SMEM(neighbours.shape, jnp.int32),
                pltpu.SMEM((3, 6 * GY), jnp.int32),
                pltpu.VMEM((bands // LANES, LANES), jnp.int32),
                *[column] * 36,
                *[pltpu.VMEM((GY, nb, LANES), jnp.float32)] * 2,
                *[column] * 2,
                *[pltpu.VMEM((YH, GY, part, LANES), bf16)] * 4,
                *[dma((GY,)), dma((2,)), dma((4,)), dma((2,))],
                *[dma((6, 2)), dma((6, 2)), dma((6, 2)), dma((6, 2, GY))],
                *[dma, dma, dma, dma, dma, dma((X, 2)), dma, dma((X - 1,)), dma((X - 1,)), dma, dma((X,))],
                *[dma((2,)), dma((2,)), dma((2,)), dma, dma, dma],
            ],
            compiler_params=pltpu.CompilerParams(collective_id=0, has_side_effects=True),
        )(start, blocks, neighbours, band_order.reshape(bands // LANES, LANES), rotation)

    return jax.shard_map(
        body,
        mesh=mesh,
        in_specs=(
            P("elem", None, "band"),
            P("elem", None, None, None),
            P("elem", None),
            P(),
            P("elem", "band"),
        ),
        out_specs=P("elem", None, "band"),
        check_vma=False,
    )


def solution(mesh):
    return build(mesh, **SIZES)
```

```python
import functools

import jax
import jax.numpy as jnp
from jax import lax
from jax.experimental import pallas as pl
from jax.experimental.pallas import tpu as pltpu
from jax.sharding import PartitionSpec as P

MESH = pl.DeviceIdType.MESH
GY = 3
LANES = 128
SIZES = dict(X=4, YL=2, Z=8, YH=4)


def kernel(X, YL, Z, YH, start, blocks, links_in, order_in, rotation, out, blk, perm, rot, racc, turned, first, links, table, order, *rest):
    bf16, f32 = jnp.bfloat16, jnp.float32
    rest = list(rest)

    def take(n):
        got, rest[:] = rest[:n], rest[n:]
        return got

    own = [take(2) for _ in range(6)]
    near = [take(2) for _ in range(6)]
    far = [take(2) for _ in range(6)]
    acc = take(2)
    filt = take(2)
    gath = take(2)
    back = take(2)
    (landed,) = take(1)
    (
        (s_blk, s_small, s_init, r_own, s_near, r_near, s_far, r_far),
        (s_z, r_z, l_rot, s_y, r_y, s_slab, r_slab, s_x, r_x, s_core, r_core),
        (s_a2a, r_a2a, l_a2a, s_out, r_out, l_out),
    ) = rest[:8], rest[8:19], rest[19:]

    E = X * YL * Z
    Y = YH * YL
    nb = blk.shape[2]
    part = nb // YH
    half = YH // 2
    elem, band = lax.axis_index("elem"), lax.axis_index("band")
    core, yh = lax.rem(band, 2), lax.div(band, 2)
    z, yl, x = lax.rem(elem, Z), lax.rem(lax.div(elem, Z), YL), lax.div(elem, Z * YL)
    y = yh * YL + yl
    twin = yh * 2 + 1 - core
    partner = (elem, twin)
    zpeer = (lax.rem(elem - 1 + 2 * core + E, E), twin)
    zother = (lax.rem(elem + 1 - 2 * core + E, E), band)
    mine, theirs = GY * core, GY * (1 - core)

    def remote(src, dst, ss, rs, dev):
        return pltpu.make_async_remote_copy(
            src_ref=src, dst_ref=dst, send_sem=ss, recv_sem=rs, device_id=dev, device_id_type=MESH
        )

    def wait(ref, sem):
        pltpu.make_async_copy(ref, ref, sem).wait()

    z_peers = [(elem - z + lax.rem(z + d, Z), band) for d in range(1, Z)]
    y_peers = []
    for d in range(1, Y):
        other = lax.rem(y + d, Y)
        y_peers.append(((x * YL + lax.rem(other, YL)) * Z + z, lax.div(other, YL) * 2 + core))
    x_peers = [((lax.rem(x + d, X) * YL + yl) * Z + z, band) for d in range(1, X)]
    a_peers = [(elem, lax.rem(yh + d, YH) * 2 + core) for d in range(1, YH)]

    barrier = pltpu.get_barrier_semaphore()
    greeted = [partner] + z_peers + y_peers + x_peers
    greeted += [(elem, lax.rem(yh + d, YH) * 2 + 1 - core) for d in range(1, YH)]
    for step in (1, E - 1):
        for c in range(2):
            greeted.append((lax.rem(elem + step, E), yh * 2 + c))
    for dev in greeted:
        pl.semaphore_signal(barrier, inc=1, device_id=dev, device_id_type=MESH)

    pltpu.make_async_copy(links_in, links, s_small.at[0]).start()
    pltpu.make_async_copy(order_in, order, s_small.at[1]).start()
    for k in range(2):

        @pl.when(core == k)
        def _():
            pltpu.make_async_copy(start.at[pl.ds(mine, GY)], own[0][k], r_own.at[k]).start()
            pltpu.make_async_copy(start.at[pl.ds(theirs, GY)], near[0][k], r_near.at[0, k]).start()

    for i in range(GY):
        pltpu.make_async_copy(blocks.at[mine + i], blk.at[i], s_blk.at[i]).start()
    wait(links, s_small.at[0])
    t_near, t_far = 2 - core, 1 + core

    def place(row, t):
        return lax.rem(links[row, t], GY)

    def slot_of(c, e):
        return e if isinstance(c, int) and c == 0 else jnp.where(c == 1, place(GY + e, 2), e)

    for j in range(GY):
        second = jnp.where(place(GY, 2) == j, 0, jnp.where(place(GY + 1, 2) == j, 1, 2))
        e = jnp.where(core == 0, j, second)
        row = mine + e
        ids = (place(row, 3), place(row, 4), place(row, t_near))
        slots = (slot_of(core, ids[0]), slot_of(core, ids[1]), slot_of(1 - core, ids[2]))
        for v, line in ((0, (e, e, *ids)), (1, (e, j, *slots))):
            for n, value in enumerate(line):
                table[v, j * 5 + n] = value
        table[2, j] = second

    for k, column in ((0, near[0][0]), (1, own[0][1])):

        @pl.when(core == k)
        def _():
            wait(own[0][k], r_own.at[k])
            wait(near[0][k], r_near.at[0, k])
            for j in range(GY):
                first[j] = column[table[2, j]]

    pl.semaphore_wait(barrier, len(greeted))

    def at_end(c):
        return jnp.logical_or(c == 0, c == Z - 1)

    end_plane = at_end(z)
    inner_plane = jnp.logical_not(end_plane)

    @pl.when(inner_plane)
    def _():
        pltpu.make_async_copy(rotation, rot.at[core, x, y, z], l_rot).start()

    def first_far(k):
        for j in range(GY):
            here = start.at[j]
            for n, (src, dev) in enumerate(((first.at[j] if k else here, zpeer), (here if k else first.at[j], zother))):
                remote(src, far[0][k].at[j], s_init.at[n], r_far.at[0, k, j], dev).start()

    for k in range(2):

        @pl.when(core == k)
        def _():
            if k == 0:
                first_far(k)
            remote(start.at[pl.ds(theirs, GY)], own[0][k], s_init.at[2], r_own.at[k], partner).start()
            remote(start.at[pl.ds(mine, GY)], near[0][k], s_init.at[3], r_near.at[0, k], partner).start()

    for d, dev in enumerate(z_peers):

        @pl.when(jnp.logical_not(at_end(lax.rem(z + d + 1, Z))))
        def _():
            remote(rotation, rot.at[core, x, y, z], s_z, r_z, dev).start()

    wait(order, s_small.at[1])

    kts, width = perm.shape[0], perm.shape[3]

    def one_hot(step, carry):
        kt, xx = lax.div(step, X), lax.rem(step, X)
        k, yp = lax.div(kt, half), lax.rem(kt, half)
        for h in range(2):
            rows = lax.broadcasted_iota(jnp.int32, (LANES, LANES), 0) + ((2 * yp + h) * 2 + k) * LANES
            for j in range(width // LANES):
                wanted = order[pl.ds(xx * (width // LANES) + j, 1), :]
                hit = jnp.where(rows == wanted, 1.0, 0.0).astype(bf16)
                perm[kt, xx, h * LANES : (h + 1) * LANES, j * LANES : (j + 1) * LANES] = hit
        return carry

    def row_of(st):
        return 0 if st == 0 else 1

    def before(st, k):
        v = row_of(st)

        def one(j, carry):
            e = table[v, j * 5]
            total = jnp.dot(blk[e, t_near], near[st][k][table[v, j * 5 + 4]], preferred_element_type=f32)
            for n, t in ((1, 0), (2, 3), (3, 4)):
                total += jnp.dot(blk[e, t], own[st][k][table[v, j * 5 + n]], preferred_element_type=f32)
            acc[k][j] = total
            return carry

        lax.fori_loop(0, GY, one, 0)

    def halo(st, k, j):
        src = own[st][k].at[j]
        remote(src, far[st][k].at[j], s_far.at[st, k], r_far.at[st, k, j], zpeer).start()
        remote(src, near[st][k].at[j], s_near.at[st, k], r_near.at[st, k], partner).start()

    def exchange(k, j):
        for d in range(1, YH):
            q = lax.rem(yh + d, YH)
            src = filt[k].at[j, pl.ds(q * part, part)]
            remote(src, gath[k].at[j, yh], s_a2a.at[k], r_a2a.at[k, j], a_peers[d - 1]).start()
        src = filt[k].at[j, pl.ds(yh * part, part)]
        pltpu.make_async_copy(src, gath[k].at[j, yh], l_a2a.at[k, j]).start()

    def after(st, k):
        v = row_of(st)
        def one(j, carry):
            e = table[v, j * 5]
            wait(far[st][k].at[j], r_far.at[st, k, j])
            total = acc[k][j] + jnp.dot(blk[e, t_far], far[st][k][j], preferred_element_type=f32)
            if st % 3:
                previous = own[st - 1][k][e if st == 1 else j]
                total = 2.0 * total - previous.astype(f32)
            if st < 5:
                own[st + 1][k][j] = total.astype(bf16)
                halo(st + 1, k, j)
            else:
                filt[k][j] = total.astype(bf16)
                exchange(k, j)
            return carry

        lax.fori_loop(0, GY, one, 0)

    def early(st, k):
        wait(near[st][k], r_near.at[st, k])
        before(st, k)

    lax.fori_loop(0, kts * X, one_hot, 0)

    @pl.when(core == 1)
    def _():
        wait(own[0][0], r_own.at[0])
        wait(near[0][0], r_near.at[0, 0])
        first_far(1)

    for i in range(GY):
        wait(blk.at[i], s_blk.at[i])
    before(0, 0)

    @pl.when(core == 0)
    def _():
        wait(own[0][1], r_own.at[1])
        wait(near[0][1], r_near.at[0, 1])

    before(0, 1)

    slab = rot.at[core, x]

    def along_y():
        wait(rot.at[core, x, y, z], l_rot)
        wait(rot.at[core, x, y, pl.ds(0, Z - 1)], r_z)
        at = rot.at[core, x, y]
        for d in range(1, Y):
            remote(at, at, s_y, r_y, y_peers[d - 1]).start()

    beside = [d for d in range(1, X) if d in (1, X - 1)]
    others = [d for d in range(1, X) if d not in beside]

    def to_end_plane(at, n, sem):
        for m, (plane, step) in enumerate(((1, -1), (Z - 2, 1))):

            @pl.when(z == plane)
            def _():
                remote(at, at, s_slab.at[n, m], sem, (elem + step, band)).start()

    def inner_spread():
        wait(rot.at[core, x, pl.ds(0, Y - 1)], r_y)
        to_end_plane(slab, 0, r_slab)
        for d in others + beside:
            remote(slab, slab, s_x.at[d - 1], r_x.at[d - 1], x_peers[d - 1]).start()
        remote(slab, slab, s_core, r_core.at[0], partner).start()

    def end_spread():
        wait(slab, r_slab)
        for d in beside:
            remote(slab, slab, s_x.at[d - 1], r_x.at[d - 1], x_peers[d - 1]).start()
        remote(slab, slab, s_core, r_core.at[0], partner).start()

    def hand_over(ds):
        for d in ds:
            at = rot.at[core, lax.rem(x - d + X, X)]
            wait(at, r_x.at[d - 1])
            remote(at, at, s_core, r_core.at[d], partner).start()
            if d in others:
                to_end_plane(at, d, r_x.at[d - 1])

    for st in range(6):
        if st == 5:
            pl.when(inner_plane)(lambda: hand_over(others))
        after(st, 0)
        if st == 1:
            pl.when(inner_plane)(along_y)
        if st == 3:
            pl.when(inner_plane)(inner_spread)
        if st:
            early(st, 1)
        after(st, 1)
        if st == 4:
            pl.when(end_plane)(end_spread)
        if st < 5:
            early(st + 1, 0)
    def reordered(k, j, xx):
        total = None
        for yp in range(half):
            both = jnp.concatenate([gath[k][j, 2 * yp + h] for h in range(2)], axis=1)
            term = jnp.dot(both, perm[k * half + yp, xx], preferred_element_type=f32)
            total = term if total is None else total + term
        return total

    def arrived(k, j):
        wait(gath[k].at[j, 0], l_a2a.at[k, j])
        wait(gath[k].at[j, pl.ds(0, YH - 1)], r_a2a.at[k, j])

    def first_half(j, carry):
        arrived(0, j)
        for xx in range(X):
            racc[j, xx] = reordered(0, j, xx)
        return carry

    def second_half(j):
        arrived(1, j)
        for xx in range(X):
            turned[j, xx] = (racc[j, xx] + reordered(1, j, xx)).astype(bf16)

    def rotate(j, m):
        goal = core if m == 0 else 1 - core
        landing = landed.at[mine + j, pl.ds(yh * part, part), :]
        for t in range(half):
            yp = lax.rem(lax.div(yh, 2) + 1 + t, half)
            total = None
            for xx in range(X):
                both = [rot[goal, xx, pl.ds((2 * yp + h) * YL, YL)].reshape(width, LANES) for h in range(2)]
                term = jnp.dot(turned[j, xx], jnp.concatenate(both, axis=1), preferred_element_type=f32)
                total = term if total is None else total + term
            total = total.astype(bf16)
            for h in range(2):
                back[m][j, 2 * yp + h] = total[:, h * LANES : (h + 1) * LANES]
            if t < half - 1:
                goals = [2 * yp, 2 * yp + 1]
            else:
                goals = [yh + 1 - 2 * lax.rem(yh, 2)]
                if m == 0:
                    pltpu.make_async_copy(back[m].at[j, yh], landing, l_out).start()
                else:
                    goals = [*goals, yh]
            for q in goals:
                remote(back[m].at[j, q], landing, s_out, r_out, (elem, q * 2 + goal)).start()

    def own_bands(j, carry):
        second_half(j)
        rotate(j, 0)
        return carry

    def other_bands(j, carry):
        rotate(j, 1)
        return carry

    lax.fori_loop(0, GY, first_half, 0)
    hand_over(beside)
    pl.when(end_plane)(lambda: hand_over(others))
    lax.fori_loop(0, GY, own_bands, 0)
    for d in range(X):
        wait(rot.at[core, 0], r_core.at[d])
    lax.fori_loop(0, GY, other_bands, 0)

    for j in range(4):
        wait(own[0][0], s_init.at[j])
    for st in range(1, 6):
        for k in range(2):
            wait(own[st][k], s_far.at[st, k])
            wait(own[st][k], s_near.at[st, k])

    @pl.when(end_plane)
    def _():
        wait(rot.at[core, x, y, pl.ds(0, Z - 2)], s_z)

    @pl.when(inner_plane)
    def _():
        wait(rot.at[core, x, y, pl.ds(0, Z - 3)], s_z)
        wait(rot.at[core, x, pl.ds(0, Y - 1)], s_y)

    for m, plane in enumerate((1, Z - 2)):

        @pl.when(z == plane)
        def _():
            for n in (0, *others):
                wait(slab, s_slab.at[n, m])

    for d in beside:
        wait(slab, s_x.at[d - 1])

    @pl.when(inner_plane)
    def _():
        for d in others:
            wait(slab, s_x.at[d - 1])

    wait(rot.at[core], s_core)
    for k in range(2):
        wait(gath[k].at[:, pl.ds(0, YH - 1)], s_a2a.at[k])
    most = landed.at[:, pl.ds(0, nb - part // 2), :]
    wait(landed.at[pl.ds(0, GY), pl.ds(0, part), :], l_out)
    wait(most, s_out)
    wait(most, r_out)
    for c in range(2):
        for i in range(GY):
            out[c * GY + i] = landed[c * GY + slot_of(c, i)]


def build(mesh, X, YL, Z, YH):
    Y = YH * YL

    def body(start, blocks, neighbours, band_order, rotation):
        nb = start.shape[1]
        bands = band_order.shape[0]
        rows = rotation.shape[0]
        part = nb // YH
        kts = YH
        bf16 = jnp.bfloat16
        column = pltpu.VMEM((GY, nb, LANES), bf16)
        dma = pltpu.SemaphoreType.DMA
        hbm = pl.BlockSpec(memory_space=pl.ANY)
        return pl.pallas_call(
            functools.partial(kernel, X, YL, Z, YH),
            out_shape=pltpu.VMEM(start.shape, bf16),
            in_specs=[hbm] * 5,
            out_specs=pl.BlockSpec(memory_space=pltpu.VMEM),
            scratch_shapes=[
                pltpu.VMEM((GY, 5, nb, nb), bf16),
                pltpu.VMEM((kts, X, 2 * LANES, bands // X), bf16),
                pltpu.VMEM((2, X, Y, Z, rows, LANES), bf16),
                pltpu.VMEM((GY, X, part, bands // X), jnp.float32),
                pltpu.VMEM((GY, X, part, bands // X), bf16),
                column,
                pltpu.SMEM(neighbours.shape, jnp.int32),
                pltpu.SMEM((3, 6 * GY), jnp.int32),
                pltpu.VMEM((bands // LANES, LANES), jnp.int32),
                *[column] * 36,
                *[pltpu.VMEM((GY, nb, LANES), jnp.float32)] * 2,
                *[column] * 2,
                *[pltpu.VMEM((GY, YH, part, LANES), bf16)] * 4,
                pltpu.VMEM(start.shape, bf16),
                *[dma((GY,)), dma((2,)), dma((4,)), dma((2,))],
                *[dma((6, 2)), dma((6, 2)), dma((6, 2)), dma((6, 2, GY))],
                *[dma, dma, dma, dma, dma, dma((X, 2)), dma, dma((X - 1,)), dma((X - 1,)), dma, dma((X,))],
                *[dma((2,)), dma((2, GY)), dma((2, GY)), dma, dma, dma],
            ],
            compiler_params=pltpu.CompilerParams(collective_id=0, has_side_effects=True),
        )(start, blocks, neighbours, band_order.reshape(bands // LANES, LANES), rotation)

    return jax.shard_map(
        body,
        mesh=mesh,
        in_specs=(
            P("elem", None, "band"),
            P("elem", None, None, None),
            P("elem", None),
            P(),
            P("elem", "band"),
        ),
        out_specs=P("elem", None, "band"),
        check_vma=False,
    )


def solution(mesh):
    return build(mesh, **SIZES)
```

```python
import functools

import jax
import jax.numpy as jnp
from jax import lax
from jax.experimental import pallas as pl
from jax.experimental.pallas import tpu as pltpu
from jax.sharding import PartitionSpec as P

MESH = pl.DeviceIdType.MESH
GY = 3
LANES = 128
SIZES = dict(X=4, YL=2, Z=8, YH=4)


def kernel(X, YL, Z, YH, start, blocks, links_in, order_in, rotation, out, blk, perm, rot, racc, turned, first, links, table, order, *rest):
    bf16, f32 = jnp.bfloat16, jnp.float32
    rest = list(rest)

    def take(n):
        got, rest[:] = rest[:n], rest[n:]
        return got

    own = [take(2) for _ in range(6)]
    near = [take(2) for _ in range(6)]
    far = [take(2) for _ in range(6)]
    acc = take(2)
    filt = take(2)
    gath = take(2)
    back = take(2)
    (landed,) = take(1)
    (
        (s_blk, s_small, s_init, r_own, s_near, r_near, s_far, r_far),
        (s_z, r_z, l_rot, s_y, r_y, s_slab, r_slab, s_x, r_x, s_core, r_core),
        (s_a2a, r_a2a, l_a2a, s_out, r_out, l_out),
    ) = rest[:8], rest[8:19], rest[19:]

    E = X * YL * Z
    Y = YH * YL
    nb = blk.shape[2]
    part = nb // YH
    half = YH // 2
    elem, band = lax.axis_index("elem"), lax.axis_index("band")
    core, yh = lax.rem(band, 2), lax.div(band, 2)
    z, yl, x = lax.rem(elem, Z), lax.rem(lax.div(elem, Z), YL), lax.div(elem, Z * YL)
    y = yh * YL + yl
    twin = yh * 2 + 1 - core
    partner = (elem, twin)
    zpeer = (lax.rem(elem - 1 + 2 * core + E, E), twin)
    zother = (lax.rem(elem + 1 - 2 * core + E, E), band)
    mine, theirs = GY * core, GY * (1 - core)

    def remote(src, dst, ss, rs, dev):
        return pltpu.make_async_remote_copy(
            src_ref=src, dst_ref=dst, send_sem=ss, recv_sem=rs, device_id=dev, device_id_type=MESH
        )

    def wait(ref, sem):
        pltpu.make_async_copy(ref, ref, sem).wait()

    z_peers = [(elem - z + lax.rem(z + d, Z), band) for d in range(1, Z)]
    y_peers = []
    for d in range(1, Y):
        other = lax.rem(y + d, Y)
        y_peers.append(((x * YL + lax.rem(other, YL)) * Z + z, lax.div(other, YL) * 2 + core))
    x_peers = [((lax.rem(x + d, X) * YL + yl) * Z + z, band) for d in range(1, X)]
    a_peers = [(elem, lax.rem(yh + d, YH) * 2 + core) for d in range(1, YH)]

    pltpu.make_async_copy(links_in, links, s_small.at[0]).start()

    barrier = pltpu.get_barrier_semaphore()
    greeted = [(lax.rem(elem + step, E), yh * 2 + c) for c in range(2) for step in (1, E - 1)]
    greeted += [partner] + z_peers + y_peers + x_peers
    greeted += [(elem, lax.rem(yh + d, YH) * 2 + 1 - core) for d in range(1, YH)]
    for dev in greeted:
        pl.semaphore_signal(barrier, inc=1, device_id=dev, device_id_type=MESH)

    pltpu.make_async_copy(order_in, order, s_small.at[1]).start()
    for k in range(2):

        @pl.when(core == k)
        def _():
            pltpu.make_async_copy(start.at[pl.ds(mine, GY)], own[0][k], r_own.at[k]).start()
            pltpu.make_async_copy(start.at[pl.ds(theirs, GY)], near[0][k], r_near.at[0, k]).start()

    for i in range(GY):
        pltpu.make_async_copy(blocks.at[mine + i], blk.at[i], s_blk.at[i]).start()
    wait(links, s_small.at[0])
    t_near, t_far = 2 - core, 1 + core

    def place(row, t):
        return lax.rem(links[row, t], GY)

    def slot_of(c, e):
        return e if isinstance(c, int) and c == 0 else jnp.where(c == 1, place(GY + e, 2), e)

    for j in range(GY):
        second = jnp.where(place(GY, 2) == j, 0, jnp.where(place(GY + 1, 2) == j, 1, 2))
        e = jnp.where(core == 0, j, second)
        row = mine + e
        ids = (place(row, 3), place(row, 4), place(row, t_near))
        slots = (slot_of(core, ids[0]), slot_of(core, ids[1]), slot_of(1 - core, ids[2]))
        for v, line in ((0, (e, e, *ids)), (1, (e, j, *slots))):
            for n, value in enumerate(line):
                table[v, j * 5 + n] = value
        table[2, j] = second

    for k, column in ((0, near[0][0]), (1, own[0][1])):

        @pl.when(core == k)
        def _():
            wait(own[0][k], r_own.at[k])
            wait(near[0][k], r_near.at[0, k])
            for j in range(GY):
                first[j] = column[table[2, j]]

    pl.semaphore_wait(barrier, len(greeted))

    def at_end(c):
        return jnp.logical_or(c == 0, c == Z - 1)

    end_plane = at_end(z)
    inner_plane = jnp.logical_not(end_plane)

    @pl.when(inner_plane)
    def _():
        pltpu.make_async_copy(rotation, rot.at[core, x, y, z], l_rot).start()

    def first_far(k):
        for j in range(GY):
            here = start.at[j]
            for n, (src, dev) in enumerate(((first.at[j] if k else here, zpeer), (here if k else first.at[j], zother))):
                remote(src, far[0][k].at[j], s_init.at[n], r_far.at[0, k, j], dev).start()

    for k in range(2):

        @pl.when(core == k)
        def _():
            if k == 0:
                first_far(k)
            remote(start.at[pl.ds(theirs, GY)], own[0][k], s_init.at[2], r_own.at[k], partner).start()
            remote(start.at[pl.ds(mine, GY)], near[0][k], s_init.at[3], r_near.at[0, k], partner).start()

    for d, dev in enumerate(z_peers):

        @pl.when(jnp.logical_not(at_end(lax.rem(z + d + 1, Z))))
        def _():
            remote(rotation, rot.at[core, x, y, z], s_z, r_z, dev).start()

    wait(order, s_small.at[1])

    kts, width = perm.shape[0], perm.shape[3]

    def one_hot(step, carry):
        kt, xx = lax.div(step, X), lax.rem(step, X)
        k, yp = lax.div(kt, half), lax.rem(kt, half)
        for h in range(2):
            rows = lax.broadcasted_iota(jnp.int32, (LANES, LANES), 0) + ((2 * yp + h) * 2 + k) * LANES
            for j in range(width // LANES):
                wanted = order[pl.ds(xx * (width // LANES) + j, 1), :]
                hit = jnp.where(rows == wanted, 1.0, 0.0).astype(bf16)
                perm[kt, xx, h * LANES : (h + 1) * LANES, j * LANES : (j + 1) * LANES] = hit
        return carry

    def row_of(st):
        return 0 if st == 0 else 1

    def before(st, k):
        v = row_of(st)

        def one(j, carry):
            e = table[v, j * 5]
            total = jnp.dot(blk[e, t_near], near[st][k][table[v, j * 5 + 4]], preferred_element_type=f32)
            for n, t in ((1, 0), (2, 3), (3, 4)):
                total += jnp.dot(blk[e, t], own[st][k][table[v, j * 5 + n]], preferred_element_type=f32)
            acc[k][j] = total
            return carry

        lax.fori_loop(0, GY, one, 0)

    def halo(st, k, j):
        src = own[st][k].at[j]
        remote(src, far[st][k].at[j], s_far.at[st, k], r_far.at[st, k, j], zpeer).start()
        remote(src, near[st][k].at[j], s_near.at[st, k], r_near.at[st, k], partner).start()

    def exchange(k, j):
        for d in sorted(range(1, YH), key=lambda d: -min(d, YH - d)):
            q = lax.rem(yh + d, YH)
            src = filt[k].at[j, pl.ds(q * part, part)]
            remote(src, gath[k].at[j, yh], s_a2a.at[k], r_a2a.at[k, j], a_peers[d - 1]).start()
        src = filt[k].at[j, pl.ds(yh * part, part)]
        pltpu.make_async_copy(src, gath[k].at[j, yh], l_a2a.at[k, j]).start()

    def after(st, k):
        v = row_of(st)
        def one(j, carry):
            e = table[v, j * 5]
            wait(far[st][k].at[j], r_far.at[st, k, j])
            total = acc[k][j] + jnp.dot(blk[e, t_far], far[st][k][j], preferred_element_type=f32)
            if st % 3:
                previous = own[st - 1][k][e if st == 1 else j]
                total = 2.0 * total - previous.astype(f32)
            if st < 5:
                own[st + 1][k][j] = total.astype(bf16)
                halo(st + 1, k, j)
            else:
                filt[k][j] = total.astype(bf16)
                exchange(k, j)
            return carry

        lax.fori_loop(0, GY, one, 0)

    def early(st, k):
        wait(near[st][k], r_near.at[st, k])
        before(st, k)

    lax.fori_loop(0, kts * X, one_hot, 0)

    @pl.when(core == 1)
    def _():
        wait(own[0][0], r_own.at[0])
        wait(near[0][0], r_near.at[0, 0])
        first_far(1)

    for i in range(GY):
        wait(blk.at[i], s_blk.at[i])
    before(0, 0)

    @pl.when(core == 0)
    def _():
        wait(own[0][1], r_own.at[1])
        wait(near[0][1], r_near.at[0, 1])

    before(0, 1)

    slab = rot.at[core, x]

    def along_y():
        wait(rot.at[core, x, y, z], l_rot)
        wait(rot.at[core, x, y, pl.ds(0, Z - 1)], r_z)
        at = rot.at[core, x, y]
        for d in range(1, Y):
            remote(at, at, s_y, r_y, y_peers[d - 1]).start()

    beside = [d for d in range(1, X) if d in (1, X - 1)]
    others = [d for d in range(1, X) if d not in beside]

    def to_end_plane(at, n, sem):
        for m, (plane, step) in enumerate(((1, -1), (Z - 2, 1))):

            @pl.when(z == plane)
            def _():
                remote(at, at, s_slab.at[n, m], sem, (elem + step, band)).start()

    def inner_spread():
        wait(rot.at[core, x, pl.ds(0, Y - 1)], r_y)
        to_end_plane(slab, 0, r_slab)
        for d in others + beside:
            remote(slab, slab, s_x.at[d - 1], r_x.at[d - 1], x_peers[d - 1]).start()
        remote(slab, slab, s_core, r_core.at[0], partner).start()

    def end_spread():
        wait(slab, r_slab)
        for d in beside:
            remote(slab, slab, s_x.at[d - 1], r_x.at[d - 1], x_peers[d - 1]).start()
        remote(slab, slab, s_core, r_core.at[0], partner).start()

    def hand_over(ds):
        for d in ds:
            at = rot.at[core, lax.rem(x - d + X, X)]
            wait(at, r_x.at[d - 1])
            remote(at, at, s_core, r_core.at[d], partner).start()
            if d in others:
                to_end_plane(at, d, r_x.at[d - 1])

    for st in range(6):
        if st == 5:
            pl.when(inner_plane)(lambda: hand_over(others))
        if st == 3:
            pl.when(inner_plane)(inner_spread)
        after(st, 0)
        if st == 1:
            pl.when(inner_plane)(along_y)
        if st:
            early(st, 1)
        after(st, 1)
        if st == 4:
            pl.when(end_plane)(end_spread)
        if st < 5:
            early(st + 1, 0)
    def reordered(k, j, xx):
        total = None
        for yp in range(half):
            both = jnp.concatenate([gath[k][j, 2 * yp + h] for h in range(2)], axis=1)
            term = jnp.dot(both, perm[k * half + yp, xx], preferred_element_type=f32)
            total = term if total is None else total + term
        return total

    def arrived(k, j):
        wait(gath[k].at[j, 0], l_a2a.at[k, j])
        wait(gath[k].at[j, pl.ds(0, YH - 1)], r_a2a.at[k, j])

    def first_half(j, carry):
        arrived(0, j)
        for xx in range(X):
            racc[j, xx] = reordered(0, j, xx)
        return carry

    def second_half(j):
        arrived(1, j)
        for xx in range(X):
            turned[j, xx] = (racc[j, xx] + reordered(1, j, xx)).astype(bf16)

    def rotate(j, m):
        goal = core if m == 0 else 1 - core
        landing = landed.at[mine + j, pl.ds(yh * part, part), :]
        for t in range(half):
            yp = lax.rem(lax.div(yh, 2) + 1 + t, half)
            total = None
            for xx in range(X):
                both = [rot[goal, xx, pl.ds((2 * yp + h) * YL, YL)].reshape(width, LANES) for h in range(2)]
                term = jnp.dot(turned[j, xx], jnp.concatenate(both, axis=1), preferred_element_type=f32)
                total = term if total is None else total + term
            total = total.astype(bf16)
            for h in range(2):
                back[m][j, 2 * yp + h] = total[:, h * LANES : (h + 1) * LANES]
            if t < half - 1:
                goals = [2 * yp, 2 * yp + 1]
            else:
                goals = [yh + 1 - 2 * lax.rem(yh, 2)]
                if m == 0:
                    pltpu.make_async_copy(back[m].at[j, yh], landing, l_out).start()
                else:
                    goals = [*goals, yh]
            for q in goals:
                remote(back[m].at[j, q], landing, s_out, r_out, (elem, q * 2 + goal)).start()

    def own_bands(j, carry):
        second_half(j)
        rotate(j, 0)
        return carry

    def other_bands(j, carry):
        rotate(j, 1)
        return carry

    lax.fori_loop(0, GY, first_half, 0)
    hand_over(beside)
    pl.when(end_plane)(lambda: hand_over(others))
    lax.fori_loop(0, GY, own_bands, 0)
    for d in range(X):
        wait(rot.at[core, 0], r_core.at[d])
    lax.fori_loop(0, GY, other_bands, 0)

    for j in range(4):
        wait(own[0][0], s_init.at[j])
    for st in range(1, 6):
        for k in range(2):
            wait(own[st][k], s_far.at[st, k])
            wait(own[st][k], s_near.at[st, k])

    @pl.when(end_plane)
    def _():
        wait(rot.at[core, x, y, pl.ds(0, Z - 2)], s_z)

    @pl.when(inner_plane)
    def _():
        wait(rot.at[core, x, y, pl.ds(0, Z - 3)], s_z)
        wait(rot.at[core, x, pl.ds(0, Y - 1)], s_y)

    for m, plane in enumerate((1, Z - 2)):

        @pl.when(z == plane)
        def _():
            for n in (0, *others):
                wait(slab, s_slab.at[n, m])

    for d in beside:
        wait(slab, s_x.at[d - 1])

    @pl.when(inner_plane)
    def _():
        for d in others:
            wait(slab, s_x.at[d - 1])

    wait(rot.at[core], s_core)
    for k in range(2):
        wait(gath[k].at[:, pl.ds(0, YH - 1)], s_a2a.at[k])
    most = landed.at[:, pl.ds(0, nb - part // 2), :]
    wait(landed.at[pl.ds(0, GY), pl.ds(0, part), :], l_out)
    wait(most, s_out)
    wait(most, r_out)
    for c in range(2):
        for i in range(GY):
            out[c * GY + i] = landed[c * GY + slot_of(c, i)]


def build(mesh, X, YL, Z, YH):
    Y = YH * YL

    def body(start, blocks, neighbours, band_order, rotation):
        nb = start.shape[1]
        bands = band_order.shape[0]
        rows = rotation.shape[0]
        part = nb // YH
        kts = YH
        bf16 = jnp.bfloat16
        column = pltpu.VMEM((GY, nb, LANES), bf16)
        dma = pltpu.SemaphoreType.DMA
        hbm = pl.BlockSpec(memory_space=pl.ANY)
        return pl.pallas_call(
            functools.partial(kernel, X, YL, Z, YH),
            out_shape=pltpu.VMEM(start.shape, bf16),
            in_specs=[hbm] * 5,
            out_specs=pl.BlockSpec(memory_space=pltpu.VMEM),
            scratch_shapes=[
                pltpu.VMEM((GY, 5, nb, nb), bf16),
                pltpu.VMEM((kts, X, 2 * LANES, bands // X), bf16),
                pltpu.VMEM((2, X, Y, Z, rows, LANES), bf16),
                pltpu.VMEM((GY, X, part, bands // X), jnp.float32),
                pltpu.VMEM((GY, X, part, bands // X), bf16),
                column,
                pltpu.SMEM(neighbours.shape, jnp.int32),
                pltpu.SMEM((3, 6 * GY), jnp.int32),
                pltpu.VMEM((bands // LANES, LANES), jnp.int32),
                *[column] * 36,
                *[pltpu.VMEM((GY, nb, LANES), jnp.float32)] * 2,
                *[column] * 2,
                *[pltpu.VMEM((GY, YH, part, LANES), bf16)] * 4,
                pltpu.VMEM(start.shape, bf16),
                *[dma((GY,)), dma((2,)), dma((4,)), dma((2,))],
                *[dma((6, 2)), dma((6, 2)), dma((6, 2)), dma((6, 2, GY))],
                *[dma, dma, dma, dma, dma, dma((X, 2)), dma, dma((X - 1,)), dma((X - 1,)), dma, dma((X,))],
                *[dma((2,)), dma((2, GY)), dma((2, GY)), dma, dma, dma],
            ],
            compiler_params=pltpu.CompilerParams(collective_id=0, has_side_effects=True),
        )(start, blocks, neighbours, band_order.reshape(bands // LANES, LANES), rotation)

    return jax.shard_map(
        body,
        mesh=mesh,
        in_specs=(
            P("elem", None, "band"),
            P("elem", None, None, None),
            P("elem", None),
            P(),
            P("elem", "band"),
        ),
        out_specs=P("elem", None, "band"),
        check_vma=False,
    )


def solution(mesh):
    return build(mesh, **SIZES)
```

```python
import functools

import jax
import jax.numpy as jnp
from jax import lax
from jax.experimental import pallas as pl
from jax.experimental.pallas import tpu as pltpu
from jax.sharding import PartitionSpec as P

MESH = pl.DeviceIdType.MESH
GY = 3
LANES = 128
SIZES = dict(X=4, YL=2, Z=8, YH=4)


def kernel(X, YL, Z, YH, start, blocks, links_in, order_in, rotation, out, blk, perm, rot, racc, turned, first, links, table, order, *rest):
    bf16, f32 = jnp.bfloat16, jnp.float32
    rest = list(rest)

    def take(n):
        got, rest[:] = rest[:n], rest[n:]
        return got

    own = [take(2) for _ in range(6)]
    near = [take(2) for _ in range(6)]
    far = [take(2) for _ in range(6)]
    acc = take(2)
    filt = take(2)
    gath = take(2)
    back = take(2)
    (landed,) = take(1)
    (
        (s_blk, s_small, s_init, r_own, s_near, r_near, s_far, r_far),
        (s_z, r_z, l_rot, s_y, r_y, s_slab, r_slab, s_x, r_x, s_core, r_core),
        (s_a2a, r_a2a, l_a2a, s_out, r_out, l_out),
    ) = rest[:8], rest[8:19], rest[19:]

    E = X * YL * Z
    Y = YH * YL
    nb = blk.shape[2]
    part = nb // YH
    half = YH // 2
    elem, band = lax.axis_index("elem"), lax.axis_index("band")
    core, yh = lax.rem(band, 2), lax.div(band, 2)
    z, yl, x = lax.rem(elem, Z), lax.rem(lax.div(elem, Z), YL), lax.div(elem, Z * YL)
    y = yh * YL + yl
    twin = yh * 2 + 1 - core
    partner = (elem, twin)
    zpeer = (lax.rem(elem - 1 + 2 * core + E, E), twin)
    zother = (lax.rem(elem + 1 - 2 * core + E, E), band)
    mine, theirs = GY * core, GY * (1 - core)

    def remote(src, dst, ss, rs, dev):
        return pltpu.make_async_remote_copy(
            src_ref=src, dst_ref=dst, send_sem=ss, recv_sem=rs, device_id=dev, device_id_type=MESH
        )

    def wait(ref, sem):
        pltpu.make_async_copy(ref, ref, sem).wait()

    z_peers = [(elem - z + lax.rem(z + d, Z), band) for d in range(1, Z)]
    y_peers = []
    for d in range(1, Y):
        other = lax.rem(y + d, Y)
        y_peers.append(((x * YL + lax.rem(other, YL)) * Z + z, lax.div(other, YL) * 2 + core))
    x_peers = [((lax.rem(x + d, X) * YL + yl) * Z + z, band) for d in range(1, X)]
    a_peers = [(elem, lax.rem(yh + d, YH) * 2 + core) for d in range(1, YH)]

    pltpu.make_async_copy(links_in, links, s_small.at[0]).start()

    barrier = pltpu.get_barrier_semaphore()
    greeted = [(lax.rem(elem + step, E), yh * 2 + c) for c in range(2) for step in (1, E - 1)]
    greeted += [partner] + z_peers + y_peers + x_peers
    greeted += [(elem, lax.rem(yh + d, YH) * 2 + 1 - core) for d in range(1, YH)]
    for dev in greeted:
        pl.semaphore_signal(barrier, inc=1, device_id=dev, device_id_type=MESH)

    pltpu.make_async_copy(order_in, order, s_small.at[1]).start()
    for k in range(2):

        @pl.when(core == k)
        def _():
            pltpu.make_async_copy(start.at[pl.ds(mine, GY)], own[0][k], r_own.at[k]).start()
            pltpu.make_async_copy(start.at[pl.ds(theirs, GY)], near[0][k], r_near.at[0, k]).start()

    for i in range(GY):
        pltpu.make_async_copy(blocks.at[mine + i], blk.at[i], s_blk.at[i]).start()
    wait(links, s_small.at[0])
    t_near, t_far = 2 - core, 1 + core

    def place(row, t):
        return lax.rem(links[row, t], GY)

    def slot_of(c, e):
        return e if isinstance(c, int) and c == 0 else jnp.where(c == 1, place(GY + e, 2), e)

    for j in range(GY):
        second = jnp.where(place(GY, 2) == j, 0, jnp.where(place(GY + 1, 2) == j, 1, 2))
        e = jnp.where(core == 0, j, second)
        row = mine + e
        ids = (place(row, 3), place(row, 4), place(row, t_near))
        slots = (slot_of(core, ids[0]), slot_of(core, ids[1]), slot_of(1 - core, ids[2]))
        for v, line in ((0, (e, e, *ids)), (1, (e, j, *slots))):
            for n, value in enumerate(line):
                table[v, j * 5 + n] = value
        table[2, j] = second

    for k, column in ((0, near[0][0]), (1, own[0][1])):

        @pl.when(core == k)
        def _():
            wait(own[0][k], r_own.at[k])
            wait(near[0][k], r_near.at[0, k])
            for j in range(GY):
                first[j] = column[table[2, j]]

    pl.semaphore_wait(barrier, len(greeted))

    def at_end(c):
        return jnp.logical_or(c == 0, c == Z - 1)

    end_plane = at_end(z)
    inner_plane = jnp.logical_not(end_plane)

    @pl.when(inner_plane)
    def _():
        pltpu.make_async_copy(rotation, rot.at[core, x, y, z], l_rot).start()

    def first_far(k):
        for j in range(GY):
            here = start.at[j]
            for n, (src, dev) in enumerate(((first.at[j] if k else here, zpeer), (here if k else first.at[j], zother))):
                remote(src, far[0][k].at[j], s_init.at[n], r_far.at[0, k, j], dev).start()

    for k in range(2):

        @pl.when(core == k)
        def _():
            if k == 0:
                first_far(k)
            remote(start.at[pl.ds(theirs, GY)], own[0][k], s_init.at[2], r_own.at[k], partner).start()
            remote(start.at[pl.ds(mine, GY)], near[0][k], s_init.at[3], r_near.at[0, k], partner).start()

    for d, dev in enumerate(z_peers):

        @pl.when(jnp.logical_not(at_end(lax.rem(z + d + 1, Z))))
        def _():
            remote(rotation, rot.at[core, x, y, z], s_z, r_z, dev).start()

    wait(order, s_small.at[1])

    kts, width = perm.shape[0], perm.shape[3]

    def one_hot(step, carry):
        kt, xx = lax.div(step, X), lax.rem(step, X)
        k, yp = lax.div(kt, half), lax.rem(kt, half)
        for h in range(2):
            rows = lax.broadcasted_iota(jnp.int32, (LANES, LANES), 0) + ((2 * yp + h) * 2 + k) * LANES
            for j in range(width // LANES):
                wanted = order[pl.ds(xx * (width // LANES) + j, 1), :]
                hit = jnp.where(rows == wanted, 1.0, 0.0).astype(bf16)
                perm[kt, xx, h * LANES : (h + 1) * LANES, j * LANES : (j + 1) * LANES] = hit
        return carry

    def row_of(st):
        return 0 if st == 0 else 1

    def before(st, k):
        v = row_of(st)

        def one(j, carry):
            e = table[v, j * 5]
            total = jnp.dot(blk[e, t_near], near[st][k][table[v, j * 5 + 4]], preferred_element_type=f32)
            for n, t in ((1, 0), (2, 3), (3, 4)):
                total += jnp.dot(blk[e, t], own[st][k][table[v, j * 5 + n]], preferred_element_type=f32)
            acc[k][j] = total
            return carry

        lax.fori_loop(0, GY, one, 0)

    def halo(st, k, j):
        src = own[st][k].at[j]
        remote(src, far[st][k].at[j], s_far.at[st, k], r_far.at[st, k, j], zpeer).start()
        remote(src, near[st][k].at[j], s_near.at[st, k], r_near.at[st, k], partner).start()

    def exchange(k, j):
        for d in sorted(range(1, YH), key=lambda d: -min(d, YH - d)):
            q = lax.rem(yh + d, YH)
            src = filt[k].at[j, pl.ds(q * part, part)]
            remote(src, gath[k].at[j, yh], s_a2a.at[k], r_a2a.at[k, j], a_peers[d - 1]).start()
        src = filt[k].at[j, pl.ds(yh * part, part)]
        pltpu.make_async_copy(src, gath[k].at[j, yh], l_a2a.at[k, j]).start()

    def after(st, k):
        v = row_of(st)
        def one(j, carry):
            e = table[v, j * 5]
            wait(far[st][k].at[j], r_far.at[st, k, j])
            total = acc[k][j] + jnp.dot(blk[e, t_far], far[st][k][j], preferred_element_type=f32)
            if st % 3:
                previous = own[st - 1][k][e if st == 1 else j]
                total = 2.0 * total - previous.astype(f32)
            if st < 5:
                own[st + 1][k][j] = total.astype(bf16)
                halo(st + 1, k, j)
            else:
                filt[k][j] = total.astype(bf16)
                exchange(k, j)
            return carry

        lax.fori_loop(0, GY, one, 0)

    def early(st, k):
        wait(near[st][k], r_near.at[st, k])
        before(st, k)

    lax.fori_loop(0, kts * X, one_hot, 0)

    @pl.when(core == 1)
    def _():
        wait(own[0][0], r_own.at[0])
        wait(near[0][0], r_near.at[0, 0])
        first_far(1)

    for i in range(GY):
        wait(blk.at[i], s_blk.at[i])
    before(0, 0)

    @pl.when(core == 0)
    def _():
        wait(own[0][1], r_own.at[1])
        wait(near[0][1], r_near.at[0, 1])

    before(0, 1)

    slab = rot.at[core, x]

    def along_y():
        wait(rot.at[core, x, y, z], l_rot)
        wait(rot.at[core, x, y, pl.ds(0, Z - 1)], r_z)
        at = rot.at[core, x, y]
        for d in range(1, Y):
            remote(at, at, s_y, r_y, y_peers[d - 1]).start()

    beside = [d for d in range(1, X) if d in (1, X - 1)]
    others = [d for d in range(1, X) if d not in beside]

    def to_end_plane(at, n, sem):
        for m, (plane, step) in enumerate(((1, -1), (Z - 2, 1))):

            @pl.when(z == plane)
            def _():
                remote(at, at, s_slab.at[n, m], sem, (elem + step, band)).start()

    def inner_spread():
        wait(rot.at[core, x, pl.ds(0, Y - 1)], r_y)
        to_end_plane(slab, 0, r_slab)
        for d in others + beside:
            remote(slab, slab, s_x.at[d - 1], r_x.at[d - 1], x_peers[d - 1]).start()
        remote(slab, slab, s_core, r_core.at[0], partner).start()

    def end_spread():
        wait(slab, r_slab)
        for d in beside:
            remote(slab, slab, s_x.at[d - 1], r_x.at[d - 1], x_peers[d - 1]).start()
        remote(slab, slab, s_core, r_core.at[0], partner).start()

    def hand_over(ds):
        for d in ds:
            at = rot.at[core, lax.rem(x - d + X, X)]
            wait(at, r_x.at[d - 1])
            remote(at, at, s_core, r_core.at[d], partner).start()
            if d in others:
                to_end_plane(at, d, r_x.at[d - 1])

    beside_end = jnp.logical_or(z == 1, z == Z - 2)
    for st in range(6):
        if st == 5:
            pl.when(jnp.logical_and(inner_plane, jnp.logical_not(beside_end)))(lambda: hand_over(others))
        if st == 3:
            pl.when(inner_plane)(inner_spread)
        after(st, 0)
        if st == 1:
            pl.when(inner_plane)(along_y)
        if st:
            early(st, 1)
        after(st, 1)
        if st == 4:
            pl.when(beside_end)(lambda: hand_over(others))
        if st < 5:
            early(st + 1, 0)
        if st == 4:
            pl.when(end_plane)(end_spread)
    def reordered(k, j, xx):
        total = None
        for yp in range(half):
            both = jnp.concatenate([gath[k][j, 2 * yp + h] for h in range(2)], axis=1)
            term = jnp.dot(both, perm[k * half + yp, xx], preferred_element_type=f32)
            total = term if total is None else total + term
        return total

    def arrived(k, j):
        wait(gath[k].at[j, 0], l_a2a.at[k, j])
        wait(gath[k].at[j, pl.ds(0, YH - 1)], r_a2a.at[k, j])

    def first_half(j, carry):
        arrived(0, j)
        for xx in range(X):
            racc[j, xx] = reordered(0, j, xx)
        return carry

    def second_half(j):
        arrived(1, j)
        for xx in range(X):
            turned[j, xx] = (racc[j, xx] + reordered(1, j, xx)).astype(bf16)

    def rotate(j, m):
        goal = core if m == 0 else 1 - core
        landing = landed.at[mine + j, pl.ds(yh * part, part), :]
        for t in range(half):
            yp = lax.rem(lax.div(yh, 2) + 1 + t, half)
            total = None
            for xx in range(X):
                both = [rot[goal, xx, pl.ds((2 * yp + h) * YL, YL)].reshape(width, LANES) for h in range(2)]
                term = jnp.dot(turned[j, xx], jnp.concatenate(both, axis=1), preferred_element_type=f32)
                total = term if total is None else total + term
            total = total.astype(bf16)
            for h in range(2):
                back[m][j, 2 * yp + h] = total[:, h * LANES : (h + 1) * LANES]
            if t < half - 1:
                goals = [2 * yp, 2 * yp + 1]
            else:
                goals = [yh + 1 - 2 * lax.rem(yh, 2)]
                if m == 0:
                    pltpu.make_async_copy(back[m].at[j, yh], landing, l_out).start()
                else:
                    goals = [*goals, yh]
            for q in goals:
                remote(back[m].at[j, q], landing, s_out, r_out, (elem, q * 2 + goal)).start()

    def own_bands(j, carry):
        second_half(j)
        rotate(j, 0)
        return carry

    def other_bands(j, carry):
        rotate(j, 1)
        return carry

    lax.fori_loop(0, GY, first_half, 0)
    hand_over(beside)
    pl.when(end_plane)(lambda: hand_over(others))
    lax.fori_loop(0, GY, own_bands, 0)
    for d in range(X):
        wait(rot.at[core, 0], r_core.at[d])
    lax.fori_loop(0, GY, other_bands, 0)

    for j in range(4):
        wait(own[0][0], s_init.at[j])
    for st in range(1, 6):
        for k in range(2):
            wait(own[st][k], s_far.at[st, k])
            wait(own[st][k], s_near.at[st, k])

    @pl.when(end_plane)
    def _():
        wait(rot.at[core, x, y, pl.ds(0, Z - 2)], s_z)

    @pl.when(inner_plane)
    def _():
        wait(rot.at[core, x, y, pl.ds(0, Z - 3)], s_z)
        wait(rot.at[core, x, pl.ds(0, Y - 1)], s_y)

    for m, plane in enumerate((1, Z - 2)):

        @pl.when(z == plane)
        def _():
            for n in (0, *others):
                wait(slab, s_slab.at[n, m])

    for d in beside:
        wait(slab, s_x.at[d - 1])

    @pl.when(inner_plane)
    def _():
        for d in others:
            wait(slab, s_x.at[d - 1])

    wait(rot.at[core], s_core)
    for k in range(2):
        wait(gath[k].at[:, pl.ds(0, YH - 1)], s_a2a.at[k])
    most = landed.at[:, pl.ds(0, nb - part // 2), :]
    wait(landed.at[pl.ds(0, GY), pl.ds(0, part), :], l_out)
    wait(most, s_out)
    wait(most, r_out)
    for c in range(2):
        for i in range(GY):
            out[c * GY + i] = landed[c * GY + slot_of(c, i)]


def build(mesh, X, YL, Z, YH):
    Y = YH * YL

    def body(start, blocks, neighbours, band_order, rotation):
        nb = start.shape[1]
        bands = band_order.shape[0]
        rows = rotation.shape[0]
        part = nb // YH
        kts = YH
        bf16 = jnp.bfloat16
        column = pltpu.VMEM((GY, nb, LANES), bf16)
        dma = pltpu.SemaphoreType.DMA
        hbm = pl.BlockSpec(memory_space=pl.ANY)
        return pl.pallas_call(
            functools.partial(kernel, X, YL, Z, YH),
            out_shape=pltpu.VMEM(start.shape, bf16),
            in_specs=[hbm] * 5,
            out_specs=pl.BlockSpec(memory_space=pltpu.VMEM),
            scratch_shapes=[
                pltpu.VMEM((GY, 5, nb, nb), bf16),
                pltpu.VMEM((kts, X, 2 * LANES, bands // X), bf16),
                pltpu.VMEM((2, X, Y, Z, rows, LANES), bf16),
                pltpu.VMEM((GY, X, part, bands // X), jnp.float32),
                pltpu.VMEM((GY, X, part, bands // X), bf16),
                column,
                pltpu.SMEM(neighbours.shape, jnp.int32),
                pltpu.SMEM((3, 6 * GY), jnp.int32),
                pltpu.VMEM((bands // LANES, LANES), jnp.int32),
                *[column] * 36,
                *[pltpu.VMEM((GY, nb, LANES), jnp.float32)] * 2,
                *[column] * 2,
                *[pltpu.VMEM((GY, YH, part, LANES), bf16)] * 4,
                pltpu.VMEM(start.shape, bf16),
                *[dma((GY,)), dma((2,)), dma((4,)), dma((2,))],
                *[dma((6, 2)), dma((6, 2)), dma((6, 2)), dma((6, 2, GY))],
                *[dma, dma, dma, dma, dma, dma((X, 2)), dma, dma((X - 1,)), dma((X - 1,)), dma, dma((X,))],
                *[dma((2,)), dma((2, GY)), dma((2, GY)), dma, dma, dma],
            ],
            compiler_params=pltpu.CompilerParams(collective_id=0, has_side_effects=True),
        )(start, blocks, neighbours, band_order.reshape(bands // LANES, LANES), rotation)

    return jax.shard_map(
        body,
        mesh=mesh,
        in_specs=(
            P("elem", None, "band"),
            P("elem", None, None, None),
            P("elem", None),
            P(),
            P("elem", "band"),
        ),
        out_specs=P("elem", None, "band"),
        check_vma=False,
    )


def solution(mesh):
    return build(mesh, **SIZES)
```
